32 devices in a mesh: inv: 2 (over y), test: 2 (over core), tx: 4 (over z), ty: 2 (over x).
Axes of the slice: x: 2, y: 2, z: 4, core: 2. Of those that a mesh axis runs over, the one named last changes fastest.
Arguments:
- log_cond: float32 [2560, 512], P(('inv', 'tx'), 'ty'), parts along dimension 0, may hold values from -3.5 to -1.7
- log_shape: float32 [2560, 512], P(('inv', 'tx'), 'ty'), parts along dimension 0, may hold values from -2.8 to -1.6
- zone_ids: int32 [2560, 512], P(('inv', 'tx'), 'ty'), parts along dimension 0, may hold values from 0 to 7
- storage: float32 [4, 8], P('inv'), parts along dimension 0, may hold values from 0.9 to 1.2
- pump_x: int32 [4, 1], P(('inv', 'test')), parts along dimension 0, may hold values from 0 to 1279
- pump_y: int32 [4, 1], P(('inv', 'test')), parts along dimension 0, may hold values from 0 to 511
- pump_rates: float32 [4, 3, 1], P(('inv', 'test')), parts along dimension 0, may hold values from -4 to -1
- obs_x: int32 [128], P('inv'), parts along dimension 0, may hold values from 0 to 1279
- obs_y: int32 [128], P('inv'), parts along dimension 0, may hold values from 0 to 511
- observed: float32 [4, 3, 64], P(('inv', 'test')), parts along dimension 0, may hold values from -6 to 6
- frac_start: float32 [4, 1280, 512], P(('inv', 'test'), 'tx', 'ty'), parts along dimension 0, may hold values from -6 to 6
- matrix_start: float32 [4, 1280, 512], P(('inv', 'test'), 'tx', 'ty'), parts along dimension 0, may hold values from -6 to 6
- frac_end: float32 [4, 1280, 512], P(('inv', 'test'), 'tx', 'ty'), parts along dimension 0, may hold values from -6 to 6
- matrix_end: float32 [4, 1280, 512], P(('inv', 'test'), 'tx', 'ty'), parts along dimension 0, may hold values from -6 to 6
Outputs:
- cond_direction: float32 [2560, 512], P(('inv', 'tx'), 'ty'), parts along dimension 0
- shape_direction: float32 [2560, 512], P(('inv', 'tx'), 'ty'), parts along dimension 0
- frac_adjoint: float32 [4, 1280, 512], P(('inv', 'test'), 'tx', 'ty'), parts along dimension 0
- matrix_adjoint: float32 [4, 1280, 512], P(('inv', 'test'), 'tx', 'ty'), parts along dimension 0
The draws below stay inside these ranges and needn't reach their ends.
There are 2 independent parts, one for each index of `inv`. The reference program is written for one: setup_inputs(seed, part) draws one part's arguments, and reference() takes and returns one part's arrays. A program takes and returns all parts, laid end to end along the dimension named above; each array names one. Nothing has to cross between parts.
All inputs are finite; a program needn't handle non-finite values.
Results may differ from the reference program's by a relative error of at most 0.0001.
Values sent between devices are 32-bit elements; how exact they have to be, the bound alone decides.
No kernel may reach another device: no remote copies, remote signals or barrier semaphores. Data moves between devices by JAX's collectives and lax.ppermute only.
A program may use at most 64 MiB of HBM per device.

```python
import math
import jax
import jax.numpy as jnp

OBS = 64
STEPS = 3
PUMPS = 1
ZONES = 8
SMOOTH = 2
TESTS = 2
NX = 1280
NY = 512


def with_ends(values, rng, smallest, largest):
    longest = values.shape.index(max(values.shape))
    spots = []
    for shift in (0, 1):
        where = [jax.random.randint(jax.random.fold_in(rng, axis), (), 0, length) for axis, length in enumerate(values.shape)]
        where[longest] = (where[longest] + shift) % values.shape[longest]
        spots.append(tuple(where))
    return values.at[spots[0]].set(smallest).at[spots[1]].set(largest)


def block_scale(own_key, dims, cuts, smallest, largest):
    gain, own = 1.0, jax.random.fold_in(own_key, 6)
    for position, blocks in cuts:
        heights = jnp.exp(jax.random.uniform(jax.random.fold_in(own, position), (blocks,), jnp.float32, smallest / len(cuts), largest / len(cuts)))
        gain = gain * jnp.repeat(heights, dims[position] // blocks).reshape([-1 if axis == position else 1 for axis in range(len(dims))])
    return gain


def normal_values(stream_key, dims, scale, most, shards=(), kind=jnp.bfloat16):
    values = scale * jax.random.normal(stream_key, dims, jnp.float32)
    if shards:
        values = values * block_scale(stream_key, dims, shards, -0.22, 0.18)
    return jnp.clip(values, -most, most).astype(kind)


def setup_inputs(seed: int = 0, part: int = 0) -> dict:
    key_of = jax.random.split(jax.random.key(seed), 15)
    own_keys = jax.random.split(jax.random.fold_in(key_of[14], part), 15)
    log_cond = jnp.clip(-3.5 + 1.8 * jax.random.uniform(own_keys[0], (NX, NY), jnp.float32) ** block_scale(own_keys[0], (NX, NY), ((0, 4), (1, 2)), -0.2, 0.2), -3.5, -1.7)
    log_shape = jnp.clip(-2.8 + 1.1999999 * jax.random.uniform(own_keys[1], (NX, NY), jnp.float32) ** block_scale(own_keys[1], (NX, NY), ((0, 4), (1, 2)), -0.2, 0.2), -2.8, -1.6)
    zone_ids = with_ends(jax.random.randint(own_keys[2], (NX, NY), 0, ZONES), jax.random.fold_in(own_keys[2], 1), 0, ZONES - 1).astype(jnp.int32)
    storage = jnp.clip(jnp.exp(jax.random.uniform(own_keys[3], (2, ZONES), jnp.float32, math.log(0.9), math.log(1.2))), 0.9, 1.2)
    pump_x = jax.random.randint(own_keys[4], (TESTS, PUMPS), 0, NX).astype(jnp.int32)
    pump_y = jax.random.randint(own_keys[5], (TESTS, PUMPS), 0, NY).astype(jnp.int32)
    pump_rates = jnp.clip(-4.0 + 3.0 * jax.random.uniform(own_keys[6], (TESTS, STEPS, PUMPS), jnp.float32) ** block_scale(own_keys[6], (TESTS, STEPS, PUMPS), ((0, 2),), -0.2, 0.2), -4.0, -1.0)
    obs_x = with_ends(jax.random.randint(own_keys[7], (OBS,), 0, NX), jax.random.fold_in(own_keys[7], 1), 0, NX - 1).astype(jnp.int32)
    obs_y = with_ends(jax.random.randint(own_keys[8], (OBS,), 0, NY), jax.random.fold_in(own_keys[8], 1), 0, NY - 1).astype(jnp.int32)
    observed = normal_values(own_keys[9], (TESTS, STEPS, OBS), 1.0, 6.0, ((0, 2),), jnp.float32)
    frac_start = normal_values(own_keys[10], (TESTS, NX, NY), 1.0, 6.0, ((0, 2), (1, 4), (2, 2)), jnp.float32)
    matrix_start = normal_values(own_keys[11], (TESTS, NX, NY), 1.0, 6.0, ((0, 2), (1, 4), (2, 2)), jnp.float32)
    frac_end = normal_values(own_keys[12], (TESTS, NX, NY), 1.0, 6.0, ((0, 2), (1, 4), (2, 2)), jnp.float32)
    matrix_end = normal_values(own_keys[13], (TESTS, NX, NY), 1.0, 6.0, ((0, 2), (1, 4), (2, 2)), jnp.float32)
    return dict(log_cond=log_cond, log_shape=log_shape, zone_ids=zone_ids, storage=storage, pump_x=pump_x, pump_y=pump_y, pump_rates=pump_rates, obs_x=obs_x, obs_y=obs_y, observed=observed, frac_start=frac_start, matrix_start=matrix_start, frac_end=frac_end, matrix_end=matrix_end)


blend_rate = 0.2

def neighbours(padded):
    return (padded[..., :-2, 1:-1], padded[..., 2:, 1:-1], padded[..., 1:-1, :-2], padded[..., 1:-1, 2:])

def flow_sum(head, conductances):
    nearby = neighbours(jnp.pad(head, 1))
    summed = jnp.zeros_like(head)
    for conductance, beside in zip(conductances, nearby):
        summed = summed + conductance * (beside - head)
    return summed

def face_links(cond):
    return [2.0 * cond * beside / (cond + beside) for beside in neighbours(jnp.pad(cond, 1))]

def misfit(log_cond, log_shape, fracture, matrix, store_frac, store_matrix, well_x, well_y, rates, obs_x, obs_y, observed, frac_end, matrix_end):
    conductances = face_links(jnp.exp(log_cond))
    shape_factor = jnp.exp(log_shape)
    summed = jnp.zeros((), log_cond.dtype)
    for step_index in range(STEPS):
        transfer = shape_factor * (fracture - matrix)
        source = jnp.zeros_like(fracture).at[well_x, well_y].add(rates[step_index])
        fracture_next = fracture + (flow_sum(fracture, conductances) - transfer + source) / store_frac
        matrix = matrix + transfer / store_matrix
        fracture = fracture_next
        mismatch = fracture[obs_x, obs_y] - observed[step_index]
        summed = summed + 0.5 * jnp.sum(mismatch * mismatch)
    return summed + jnp.sum(frac_end * fracture) + jnp.sum(matrix_end * matrix)

def smooth(grad_field):
    for sweep_index in range(SMOOTH):
        nearby = neighbours(jnp.pad(grad_field, 1))
        grad_field = grad_field + blend_rate * (nearby[0] + nearby[1] + nearby[2] + nearby[3] - 4.0 * grad_field)
    return grad_field

def reference(log_cond, log_shape, zone_ids, storage, pump_x, pump_y, pump_rates, obs_x, obs_y, observed, frac_start, matrix_start, frac_end, matrix_end):
    store_frac = storage[0][zone_ids]
    store_matrix = storage[1][zone_ids]
    grad_cond = jnp.zeros_like(log_cond)
    grad_shape = jnp.zeros_like(log_shape)
    frac_list = []
    matrix_list = []
    for test_index in range(TESTS):
        derivatives = jax.grad(misfit, argnums=(0, 1, 2, 3))(log_cond, log_shape, frac_start[test_index], matrix_start[test_index], store_frac, store_matrix, pump_x[test_index], pump_y[test_index], pump_rates[test_index], obs_x, obs_y, observed[test_index], frac_end[test_index], matrix_end[test_index])
        grad_cond = grad_cond + derivatives[0]
        grad_shape = grad_shape + derivatives[1]
        frac_list.append(derivatives[2])
        matrix_list.append(derivatives[3])
    return (smooth(grad_cond), smooth(grad_shape), jnp.stack(frac_list), jnp.stack(matrix_list))
```

```python
import jax
import jax.numpy as jnp
from jax import lax
from jax.experimental import pallas as pl
from jax.experimental.pallas import tpu as pltpu
from jax.sharding import PartitionSpec as P

SMOOTH = 2
EDGE = 8
LANES = 128
BLEND = 0.2
FIELDS = 7


def pairs_of(count, parity):
    found = []
    for low in range(parity, count - 1, 2):
        found += [(low, low + 1), (low + 1, low)]
    return found


def rounds_of(count):
    return [parity for parity in (0, 1) if pairs_of(count, parity)]


def partner(index, parity):
    return index + 1 if index % 2 == parity else index - 1


def corner_pairs(nx, ny, px, py):
    found = []
    for x in range(nx):
        for y in range(ny):
            there = (partner(x, px), partner(y, py))
            if 0 <= there[0] < nx and 0 <= there[1] < ny:
                found.append((x * ny + y, there[0] * ny + there[1]))
    return found


def forward_of(axis, parity):
    return lax.rem(lax.axis_index(axis), 2) == parity


def lane_iota(rows, cols):
    return lax.broadcasted_iota(jnp.int32, (rows, cols), 1)


def pack(fields, xr, yr):
    tile_rows, tile_cols = fields[0].shape
    half = tile_rows // 2
    nxr, nyr = len(xr), len(yr)

    def kernel(*refs):
        ins = refs[:FIELDS]
        row_out = refs[FIELDS : FIELDS + nxr]
        col_out = refs[FIELDS + nxr : FIELDS + nxr + nyr]
        corner_out = refs[FIELDS + nxr + nyr : FIELDS + nxr + nyr + nxr * nyr]
        rest = refs[FIELDS + nxr + nyr + nxr * nyr :]
        zone_rows, cols, zone_cols, row_sem, col_sem = rest
        row_copies = []
        for i, px in enumerate(xr):
            start = jnp.where(forward_of("tx", px), tile_rows - EDGE, 0)
            start = pl.multiple_of(start, EDGE)
            for f in range(FIELDS):
                into = zone_rows.at[i] if f == 2 else row_out[i].at[pl.ds(EDGE * f, EDGE)]
                row_copies.append(
                    pltpu.make_async_copy(
                        ins[f].at[pl.ds(start, EDGE)], into, row_sem.at[i, f]
                    )
                )
        col_copies = []
        for j, py in enumerate(yr):
            start = jnp.where(forward_of("ty", py), tile_cols - LANES, 0)
            start = pl.multiple_of(start, LANES)
            for f in range(FIELDS):
                into = zone_cols.at[j] if f == 2 else cols.at[j, f]
                col_copies.append(
                    pltpu.make_async_copy(
                        ins[f].at[:, pl.ds(start, LANES)], into, col_sem.at[j, f]
                    )
                )
        for copy in row_copies + col_copies:
            copy.start()
        for copy in row_copies:
            copy.wait()
        for i in range(nxr):
            row_out[i][2 * EDGE : 3 * EDGE, :] = zone_rows[i].astype(jnp.float32)
        slot = lane_iota(EDGE, LANES) // EDGE
        for i in range(nxr):
            for j, py in enumerate(yr):
                ahead = forward_of("ty", py)
                shift = jnp.where(ahead, 1, 0)
                total = jnp.zeros((EDGE, LANES), jnp.float32)
                for f in range(FIELDS):
                    rows = row_out[i][EDGE * f : EDGE * (f + 1), :]
                    part = jnp.where(ahead, rows[:, tile_cols - LANES :], rows[:, :LANES])
                    part = pltpu.roll(part, EDGE * f, 1)
                    want = lax.rem(f - shift + 16, 16)
                    total = jnp.where(slot == want, part, total)
                corner_out[i * nyr + j][...] = total
        for copy in col_copies:
            copy.wait()
        for j, py in enumerate(yr):
            shift = jnp.where(forward_of("ty", py), 1, 0)

            def body(k, carry):
                total = jnp.zeros((EDGE, LANES), jnp.float32)
                for h in range(2):
                    at = pl.multiple_of(k * EDGE + h * half, EDGE)
                    for f in range(FIELDS):
                        if f == 2:
                            part = zone_cols[j, pl.ds(at, EDGE), :].astype(jnp.float32)
                        else:
                            part = cols[j, f, pl.ds(at, EDGE), :]
                        amount = EDGE * f + 64 * h
                        part = pltpu.roll(part, amount, 1) if amount else part
                        want = lax.rem(f + 8 * h - shift + 16, 16)
                        total = jnp.where(slot == want, part, total)
                col_out[j][pl.ds(pl.multiple_of(k * EDGE, EDGE), EDGE), :] = total
                return carry

            lax.fori_loop(0, half // EDGE, body, 0, unroll=2)

    outs = [jax.ShapeDtypeStruct((EDGE * FIELDS, tile_cols), jnp.float32)] * nxr
    outs += [jax.ShapeDtypeStruct((half, LANES), jnp.float32)] * nyr
    outs += [jax.ShapeDtypeStruct((EDGE, LANES), jnp.float32)] * (nxr * nyr)
    made = pl.pallas_call(
        kernel,
        out_shape=outs,
        in_specs=[pl.BlockSpec(memory_space=pl.ANY)] * FIELDS,
        scratch_shapes=[
            pltpu.VMEM((nxr, EDGE, tile_cols), jnp.int32),
            pltpu.VMEM((nyr, FIELDS, tile_rows, LANES), jnp.float32),
            pltpu.VMEM((nyr, tile_rows, LANES), jnp.int32),
            pltpu.SemaphoreType.DMA((nxr, FIELDS)),
            pltpu.SemaphoreType.DMA((nyr, FIELDS)),
        ],
        name="pack",
    )(*fields)
    return made[:nxr], made[nxr : nxr + nyr], made[nxr + nyr :]


def window(fields, scalars, row_in, col_in, corner_in, xr, yr, nx, ny):
    tile_rows, tile_cols = fields[0].shape
    storage, pump_x, pump_y, pump_rates, obs_x, obs_y, observed = scalars
    zones = storage.shape[1]
    steps, pumps = pump_rates.shape
    wells = obs_x.shape[0]
    assert 2 * steps + SMOOTH <= EDGE
    half = tile_rows // 2
    nxr, nyr = len(xr), len(yr)
    rows, cols = tile_rows + 2 * EDGE, tile_cols + LANES
    chunks = rows // EDGE
    f32 = jnp.float32

    def kernel(*refs):
        pos = 0

        def take(count):
            nonlocal pos
            pos += count
            return refs[pos - count : pos]

        (st, pxs, pys, prs, oxs, oys, obs) = take(7)
        ins = take(FIELDS)
        rin, cin, kin = take(nxr), take(nyr), take(nxr * nyr)
        smooth_out, frac_out, mat_out = take(3)
        (wide, zone_mid, colbuf, cornerbuf, rowzone) = take(5)
        (rm, cx, cy, count, seen, frac, fluxx, fluxy, moved, px_, py_, gs_, grad, grad2) = take(14)
        (mid_sem, row_sem, col_sem, corner_sem) = take(4)
        res, shp, rs = wide.at[0], wide.at[1], wide.at[2]
        mat, adj, adm = wide.at[4], wide.at[5], wide.at[6]

        tx, ty = lax.axis_index("tx"), lax.axis_index("ty")
        copies = []
        for f in range(FIELDS):
            into = (
                zone_mid
                if f == 2
                else (frac.at[0] if f == 3 else wide.at[f]).at[pl.ds(EDGE, tile_rows), pl.ds(0, tile_cols)]
            )
            copies.append(pltpu.make_async_copy(ins[f], into, mid_sem.at[f]))
        for j in range(nyr):
            copies.append(pltpu.make_async_copy(cin[j], colbuf.at[j], col_sem.at[j]))
        for i in range(nxr * nyr):
            copies.append(pltpu.make_async_copy(kin[i], cornerbuf.at[i], corner_sem.at[i]))
        tops = []
        for i, px in enumerate(xr):
            to = jnp.where(forward_of("tx", px), tile_rows + EDGE, 0)
            to = pl.multiple_of(to, EDGE)
            tops.append(to)
            for f in range(FIELDS):
                target = frac.at[0] if f == 3 else wide.at[f]
                copies.append(
                    pltpu.make_async_copy(
                        rin[i].at[pl.ds(EDGE * f, EDGE)],
                        target.at[pl.ds(to, EDGE), pl.ds(0, tile_cols)],
                        row_sem.at[i, f],
                    )
                )
        if nxr < 2:
            for f in range(FIELDS):
                target = frac.at[0] if f == 3 else wide.at[f]
                target[0:EDGE, :] = jnp.zeros((EDGE, cols), f32)
                target[rows - EDGE : rows, :] = jnp.zeros((EDGE, cols), f32)
        for copy in copies:
            copy.start()

        lane = lane_iota(EDGE, cols)
        col = jnp.where(lane < tile_cols + LANES // 2, lane, lane - cols)
        gcol = col + ty * tile_cols
        total_cols, total_rows = tile_cols * ny, tile_rows * nx
        col_in_grid = (gcol >= 0) & (gcol < total_cols)
        col_face = (gcol >= 0) & (gcol + 1 < total_cols)
        sub = lax.broadcasted_iota(jnp.int32, (EDGE, cols), 0)
        row0 = tx * tile_rows - EDGE

        zero = jnp.zeros((EDGE, cols), f32)

        def clear(k, carry):
            at = pl.ds(pl.multiple_of(k * EDGE, EDGE), EDGE)
            count[at, :] = zero
            for n in range(steps):
                seen[n, at, :] = zero
            return carry

        lax.fori_loop(0, chunks, clear, 0, unroll=2)
        one_lane = lane_iota(1, cols)

        def place(gx, gy):
            lr = gx - row0
            lc = gy - ty * tile_cols
            ok = (lr >= 0) & (lr < rows) & (lc >= -EDGE) & (lc < tile_cols + EDGE)
            return lr, jnp.where(lc < 0, lc + cols, lc), ok

        def well(o, carry):
            lr, ll, ok = place(oxs[o], oys[o])

            @pl.when(ok)
            def _():
                hit = one_lane == ll
                at = pl.ds(lr, 1)
                count[at, :] += jnp.where(hit, 1.0, 0.0)
                for n in range(steps):
                    seen[n, at, :] += jnp.where(hit, obs[n, o], 0.0)

            return carry

        lax.fori_loop(0, wells, well, 0)

        for copy in copies:
            copy.wait()

        def widen(k, carry):
            at = pl.ds(pl.multiple_of((k + 1) * EDGE, EDGE), EDGE)
            wide[2, at, 0:tile_cols] = zone_mid[pl.ds(pl.multiple_of(k * EDGE, EDGE), EDGE), :].astype(f32)
            return carry

        lax.fori_loop(0, tile_rows // EDGE, widen, 0, unroll=4)
        edge_lane = lane_iota(EDGE, LANES)
        side = []
        for py in yr:
            ahead = forward_of("ty", py)
            low = jnp.where(ahead, 0, LANES - EDGE)
            side.append((edge_lane >= low) & (edge_lane < low + EDGE))

        def edge_of(messages, amount):
            out = jnp.zeros((EDGE, LANES), f32)
            for mask, message in zip(side, messages):
                part = pltpu.roll(message, (LANES - amount) % LANES, 1) if amount % LANES else message
                out = jnp.where(mask, part, out)
            return out

        def put_edge(f, at, value):
            target = frac.at[0] if f == 3 else wide.at[f]
            target[at, tile_cols:cols] = value

        for h in range(2):

            def fringe(k, carry):
                src = pl.ds(pl.multiple_of(k * EDGE, EDGE), EDGE)
                at = pl.ds(pl.multiple_of(k * EDGE + EDGE + h * half, EDGE), EDGE)
                messages = [colbuf[j, src, :] for j in range(nyr)]
                for f in range(FIELDS):
                    put_edge(f, at, edge_of(messages, EDGE * f + 64 * h))
                return carry

            lax.fori_loop(0, half // EDGE, fringe, 0, unroll=2)
        for i in range(nxr):
            messages = [cornerbuf[i * nyr + j] for j in range(nyr)]
            for f in range(FIELDS):
                put_edge(f, pl.ds(tops[i], EDGE), edge_of(messages, EDGE * f))

        def at_of(k):
            return pl.ds(pl.multiple_of(k * EDGE, EDGE), EDGE)

        def next_of(k):
            return at_of(jnp.minimum(k + 1, chunks - 1))

        def up1(x):
            return pltpu.roll(x, EDGE - 1, 0)

        def down1(x):
            return pltpu.roll(x, 1, 0)

        def right(x):
            return pltpu.roll(x, cols - 1, 1)

        def left(x):
            return pltpu.roll(x, 1, 1)

        last, first = sub == EDGE - 1, sub == 0
        inv_f = [1.0 / jnp.full((EDGE, cols), st[0, z], f32) for z in range(zones)]
        inv_m = [1.0 / jnp.full((EDGE, cols), st[1, z], f32) for z in range(zones)]

        def prepare(k, carry):
            at = at_of(k)
            res[at, :] = jnp.exp(-res[at, :])
            shp[at, :] = jnp.exp(shp[at, :])
            zone = rs[at, :]
            a, b = inv_f[0], inv_m[0]
            for z in range(1, zones):
                hit = zone == float(z)
                a = jnp.where(hit, inv_f[z], a)
                b = jnp.where(hit, inv_m[z], b)
            rs[at, :] = a
            rm[at, :] = b
            return carry

        lax.fori_loop(0, chunks, prepare, 0)

        def links(k, carry):
            at = at_of(k)
            here = res[at, :]
            below = jnp.where(last, up1(res[next_of(k), :]), up1(here))
            beside = right(here)
            grow = row0 + k * EDGE + sub
            ok = (grow >= 0) & (grow + 1 < total_rows)
            cx[at, :] = jnp.where(ok, 2.0 / (here + below), 0.0)
            cy[at, :] = jnp.where(col_face, 2.0 / (here + beside), 0.0)
            return carry

        lax.fori_loop(0, chunks, links, 0, unroll=2)

        for n in range(steps):
            src, dst = frac.at[n], frac.at[n + 1]

            def step(k, carry, src=src, dst=dst, n=n):
                f, fup, flux_above = carry
                at = at_of(k)
                f_next = src[next_of(k), :]
                fup_next = up1(f_next)
                m = mat[at, :]
                fx = cx[at, :] * (jnp.where(last, fup_next, fup) - f)
                fy = cy[at, :] * (right(f) - f)
                fx_down = down1(fx)
                flow = fx - jnp.where(first, flux_above, fx_down) + fy - left(fy)
                t = shp[at, :] * (f - m)
                dst[at, :] = f + (flow - t) * rs[at, :]
                mat[at, :] = m + t * rm[at, :]
                fluxx[n, at, :] = fx
                fluxy[n, at, :] = fy
                moved[n, at, :] = t
                return f_next, fup_next, fx_down

            f0 = src[0:EDGE, :]
            lax.fori_loop(0, chunks, step, (f0, up1(f0), zero), unroll=2)
            for p in range(pumps):
                lr, ll, ok = place(pxs[0, p], pys[0, p])

                @pl.when(ok)
                def _(lr=lr, ll=ll, p=p, n=n, dst=dst):
                    at = pl.ds(lr, 1)
                    dst[at, :] += jnp.where(one_lane == ll, prs[n, p], 0.0) * rs[at, :]

        for n in reversed(range(steps)):
            opening, closing = n == steps - 1, n == 0

            def load(at, n=n):
                a = adj[at, :] + (count[at, :] * frac[n + 1, at, :] - seen[n, at, :])
                return a, a * rs[at, :]

            def back(k, carry, n=n, opening=opening, closing=closing, load=load):
                a, s, sup, flux_above, prod_above = carry
                at = at_of(k)
                a_next, s_next = load(next_of(k))
                sup_next = up1(s_next)
                sx = cx[at, :] * (jnp.where(last, sup_next, sup) - s)
                sy = cy[at, :] * (right(s) - s)
                sx_down = down1(sx)
                flow = sx - jnp.where(first, flux_above, sx_down) + sy - left(sy)
                am = adm[at, :]
                q = am * rm[at, :] - s
                swap = shp[at, :] * q
                gx = fluxx[n, at, :] * sx
                gy = fluxy[n, at, :] * sy
                gs = moved[n, at, :] * q
                if not opening:
                    gx += px_[at, :]
                    gy += py_[at, :]
                    gs += gs_[at, :]
                a_new = a + flow + swap
                am_new = am - swap
                adj[at, :] = a_new
                adm[at, :] = am_new
                if closing:
                    gx_down = down1(gx)
                    total = gx + jnp.where(first, prod_above, gx_down) + gy + left(gy)
                    grow = row0 + k * EDGE + sub
                    inside = (grow >= 0) & (grow < total_rows) & col_in_grid
                    grad[0, at, :] = jnp.where(inside, -0.5 * res[at, :] * total, 0.0)
                    grad[1, at, :] = jnp.where(inside, gs, 0.0)
                else:
                    gx_down = prod_above
                    px_[at, :] = gx
                    py_[at, :] = gy
                    gs_[at, :] = gs
                return a_next, s_next, sup_next, sx_down, gx_down

            a0, s0 = load(pl.ds(0, EDGE))
            lax.fori_loop(0, chunks, back, (a0, s0, up1(s0), zero, zero))

        out_copies = [
            pltpu.make_async_copy(
                adj.at[pl.ds(EDGE, tile_rows), pl.ds(0, tile_cols)], frac_out, mid_sem.at[0]
            ),
            pltpu.make_async_copy(
                adm.at[pl.ds(EDGE, tile_rows), pl.ds(0, tile_cols)], mat_out, mid_sem.at[1]
            ),
        ]
        for copy in out_copies:
            copy.start()

        def blur(source, q, k, g, gup, above):
            g_next = source[q, next_of(k), :]
            gup_next = up1(g_next)
            g_down = down1(g)
            around = jnp.where(last, gup_next, gup) + jnp.where(first, above, g_down)
            around = around + left(g) + right(g)
            return g + BLEND * (around - 4.0 * g), (g_next, gup_next, g_down)

        for q in range(2):

            def first_pass(k, carry, q=q):
                value, carry = blur(grad, q, k, *carry)
                grow = row0 + k * EDGE + sub
                inside = (grow >= 0) & (grow < total_rows) & col_in_grid
                grad2[q, at_of(k), :] = jnp.where(inside, value, 0.0)
                return carry

            g0 = grad[q, 0:EDGE, :]
            lax.fori_loop(0, chunks, first_pass, (g0, up1(g0), zero), unroll=2)

            def second_pass(k, carry, q=q):
                value, carry = blur(grad2, q, k, *carry)
                at = pl.ds(pl.multiple_of((k - 1) * EDGE, EDGE), EDGE)
                smooth_out[q, at, :] = value[:, 0:tile_cols]
                return carry

            g0 = grad2[q, EDGE : 2 * EDGE, :]
            lax.fori_loop(
                1,
                chunks - 1,
                second_pass,
                (g0, up1(g0), down1(grad2[q, 0:EDGE, :])),
                unroll=2,
            )
        for copy in out_copies:
            copy.wait()

    smem = pl.BlockSpec(memory_space=pltpu.SMEM)
    hbm = pl.BlockSpec(memory_space=pl.ANY)
    big = (rows, cols)
    return pl.pallas_call(
        kernel,
        out_shape=[
            jax.ShapeDtypeStruct((2, tile_rows, tile_cols), f32),
            jax.ShapeDtypeStruct((tile_rows, tile_cols), f32),
            jax.ShapeDtypeStruct((tile_rows, tile_cols), f32),
        ],
        in_specs=[smem] * 7 + [hbm] * (FIELDS + nxr + nyr + nxr * nyr),
        out_specs=[pl.BlockSpec(memory_space=pltpu.VMEM), hbm, hbm],
        scratch_shapes=[
            pltpu.VMEM((FIELDS,) + big, f32),
            pltpu.VMEM((tile_rows, tile_cols), jnp.int32),
            pltpu.VMEM((max(nyr, 1), half, LANES), f32),
            pltpu.VMEM((max(nxr * nyr, 1), EDGE, LANES), f32),
            pltpu.VMEM((EDGE, LANES), f32),
            pltpu.VMEM(big, f32),
            pltpu.VMEM(big, f32),
            pltpu.VMEM(big, f32),
            pltpu.VMEM(big, f32),
            pltpu.VMEM((steps,) + big, f32),
            pltpu.VMEM((steps + 1,) + big, f32),
            pltpu.VMEM((steps,) + big, f32),
            pltpu.VMEM((steps,) + big, f32),
            pltpu.VMEM((steps,) + big, f32),
            pltpu.VMEM(big, f32),
            pltpu.VMEM(big, f32),
            pltpu.VMEM(big, f32),
            pltpu.VMEM((2,) + big, f32),
            pltpu.VMEM((2,) + big, f32),
            pltpu.SemaphoreType.DMA((FIELDS,)),
            pltpu.SemaphoreType.DMA((nxr, FIELDS)),
            pltpu.SemaphoreType.DMA((max(nyr, 1),)),
            pltpu.SemaphoreType.DMA((max(nxr * nyr, 1),)),
        ],
        name="window",
    )(*scalars, *fields, *row_in, *col_in, *corner_in)


def on_device(
    log_cond,
    log_shape,
    zone_ids,
    storage,
    pump_x,
    pump_y,
    pump_rates,
    obs_x,
    obs_y,
    observed,
    frac_start,
    matrix_start,
    frac_end,
    matrix_end,
):
    nx, ny = lax.axis_size("tx"), lax.axis_size("ty")
    xr, yr = rounds_of(nx), rounds_of(ny)
    fields = (
        log_cond,
        log_shape,
        zone_ids,
        frac_start[0],
        matrix_start[0],
        frac_end[0],
        matrix_end[0],
    )
    row_out, col_out, corner_out = pack(fields, xr, yr)
    col_in = [lax.ppermute(m, "ty", pairs_of(ny, py)) for m, py in zip(col_out, yr)]
    row_in = [lax.ppermute(m, "tx", pairs_of(nx, px)) for m, px in zip(row_out, xr)]
    corner_in = [
        lax.ppermute(corner_out[i * len(yr) + j], ("tx", "ty"), corner_pairs(nx, ny, px, py))
        for i, px in enumerate(xr)
        for j, py in enumerate(yr)
    ]
    scalars = (storage, pump_x, pump_y, pump_rates[0], obs_x, obs_y, observed[0])
    smoothed, fracture_adj, matrix_adj = window(
        fields, scalars, row_in, col_in, corner_in, xr, yr, nx, ny
    )
    tests = lax.axis_size("test")
    summed = smoothed
    if tests == 2:
        summed = smoothed + lax.ppermute(smoothed, "test", [(0, 1), (1, 0)])
    else:
        summed = lax.psum(smoothed, "test")
    return (summed[0], summed[1], fracture_adj[None], matrix_adj[None])


def solution(mesh):
    placed = (
        P(("inv", "tx"), "ty"),
        P(("inv", "tx"), "ty"),
        P(("inv", "tx"), "ty"),
        P("inv", None),
        P(("inv", "test"), None),
        P(("inv", "test"), None),
        P(("inv", "test"), None, None),
        P("inv"),
        P("inv"),
        P(("inv", "test"), None, None),
        P(("inv", "test"), "tx", "ty"),
        P(("inv", "test"), "tx", "ty"),
        P(("inv", "test"), "tx", "ty"),
        P(("inv", "test"), "tx", "ty"),
    )
    return jax.shard_map(
        on_device,
        mesh=mesh,
        in_specs=placed,
        out_specs=(
            P(("inv", "tx"), "ty"),
            P(("inv", "tx"), "ty"),
            P(("inv", "test"), "tx", "ty"),
            P(("inv", "test"), "tx", "ty"),
        ),
        check_vma=False,
    )
```

```python
import jax
import jax.numpy as jnp
from jax import lax
from jax.experimental import pallas as pl
from jax.experimental.pallas import tpu as pltpu
from jax.sharding import PartitionSpec as P

SMOOTH = 2
EDGE = 8
LANES = 128
BLEND = 0.2
FIELDS = 7


def pairs_of(count, parity):
    found = []
    for low in range(parity, count - 1, 2):
        found += [(low, low + 1), (low + 1, low)]
    return found


def rounds_of(count):
    return [parity for parity in (0, 1) if pairs_of(count, parity)]


def partner(index, parity):
    return index + 1 if index % 2 == parity else index - 1


def corner_pairs(nx, ny, px, py):
    found = []
    for x in range(nx):
        for y in range(ny):
            there = (partner(x, px), partner(y, py))
            if 0 <= there[0] < nx and 0 <= there[1] < ny:
                found.append((x * ny + y, there[0] * ny + there[1]))
    return found


def forward_of(axis, parity):
    return lax.rem(lax.axis_index(axis), 2) == parity


def lane_iota(rows, cols):
    return lax.broadcasted_iota(jnp.int32, (rows, cols), 1)


def pack(fields, xr, yr):
    tile_rows, tile_cols = fields[0].shape
    half = tile_rows // 2
    nxr, nyr = len(xr), len(yr)

    def kernel(*refs):
        ins = refs[:FIELDS]
        row_out = refs[FIELDS : FIELDS + nxr]
        col_out = refs[FIELDS + nxr : FIELDS + nxr + nyr]
        corner_out = refs[FIELDS + nxr + nyr : FIELDS + nxr + nyr + nxr * nyr]
        rest = refs[FIELDS + nxr + nyr + nxr * nyr :]
        zone_rows, cols, zone_cols, row_sem, col_sem = rest
        row_copies = []
        for i, px in enumerate(xr):
            start = jnp.where(forward_of("tx", px), tile_rows - EDGE, 0)
            start = pl.multiple_of(start, EDGE)
            for f in range(FIELDS):
                into = zone_rows.at[i] if f == 2 else row_out[i].at[pl.ds(EDGE * f, EDGE)]
                row_copies.append(
                    pltpu.make_async_copy(
                        ins[f].at[pl.ds(start, EDGE)], into, row_sem.at[i, f]
                    )
                )
        col_copies = []
        for j, py in enumerate(yr):
            start = jnp.where(forward_of("ty", py), tile_cols - LANES, 0)
            start = pl.multiple_of(start, LANES)
            for f in range(FIELDS):
                into = zone_cols.at[j] if f == 2 else cols.at[j, f]
                col_copies.append(
                    pltpu.make_async_copy(
                        ins[f].at[:, pl.ds(start, LANES)], into, col_sem.at[j, f]
                    )
                )
        for copy in row_copies + col_copies:
            copy.start()
        for copy in row_copies:
            copy.wait()
        for i in range(nxr):
            row_out[i][2 * EDGE : 3 * EDGE, :] = zone_rows[i].astype(jnp.float32)
        slot = lane_iota(EDGE, LANES) // EDGE
        for i in range(nxr):
            for j, py in enumerate(yr):
                ahead = forward_of("ty", py)
                shift = jnp.where(ahead, 1, 0)
                total = jnp.zeros((EDGE, LANES), jnp.float32)
                for f in range(FIELDS):
                    rows = row_out[i][EDGE * f : EDGE * (f + 1), :]
                    part = jnp.where(ahead, rows[:, tile_cols - LANES :], rows[:, :LANES])
                    part = pltpu.roll(part, EDGE * f, 1)
                    want = lax.rem(f - shift + 16, 16)
                    total = jnp.where(slot == want, part, total)
                corner_out[i * nyr + j][...] = total
        for copy in col_copies:
            copy.wait()
        for j, py in enumerate(yr):
            shift = jnp.where(forward_of("ty", py), 1, 0)

            def body(k, carry):
                total = jnp.zeros((EDGE, LANES), jnp.float32)
                for h in range(2):
                    at = pl.multiple_of(k * EDGE + h * half, EDGE)
                    for f in range(FIELDS):
                        if f == 2:
                            part = zone_cols[j, pl.ds(at, EDGE), :].astype(jnp.float32)
                        else:
                            part = cols[j, f, pl.ds(at, EDGE), :]
                        amount = EDGE * f + 64 * h
                        part = pltpu.roll(part, amount, 1) if amount else part
                        want = lax.rem(f + 8 * h - shift + 16, 16)
                        total = jnp.where(slot == want, part, total)
                col_out[j][pl.ds(pl.multiple_of(k * EDGE, EDGE), EDGE), :] = total
                return carry

            lax.fori_loop(0, half // EDGE, body, 0, unroll=half // EDGE)

    outs = [jax.ShapeDtypeStruct((EDGE * FIELDS, tile_cols), jnp.float32)] * nxr
    outs += [jax.ShapeDtypeStruct((half, LANES), jnp.float32)] * nyr
    outs += [jax.ShapeDtypeStruct((EDGE, LANES), jnp.float32)] * (nxr * nyr)
    made = pl.pallas_call(
        kernel,
        out_shape=outs,
        in_specs=[pl.BlockSpec(memory_space=pl.ANY)] * FIELDS,
        scratch_shapes=[
            pltpu.VMEM((nxr, EDGE, tile_cols), jnp.int32),
            pltpu.VMEM((nyr, FIELDS, tile_rows, LANES), jnp.float32),
            pltpu.VMEM((nyr, tile_rows, LANES), jnp.int32),
            pltpu.SemaphoreType.DMA((nxr, FIELDS)),
            pltpu.SemaphoreType.DMA((nyr, FIELDS)),
        ],
        name="pack",
    )(*fields)
    return made[:nxr], made[nxr : nxr + nyr], made[nxr + nyr :]


def window(fields, scalars, row_in, col_in, corner_in, xr, yr, nx, ny):
    tile_rows, tile_cols = fields[0].shape
    storage, pump_x, pump_y, pump_rates, obs_x, obs_y, observed = scalars
    zones = storage.shape[1]
    steps, pumps = pump_rates.shape
    wells = obs_x.shape[0]
    assert 2 * steps + SMOOTH <= EDGE
    half = tile_rows // 2
    nxr, nyr = len(xr), len(yr)
    rows, cols = tile_rows + 2 * EDGE, tile_cols + LANES
    chunks = rows // EDGE
    f32 = jnp.float32

    def kernel(*refs):
        pos = 0

        def take(count):
            nonlocal pos
            pos += count
            return refs[pos - count : pos]

        (st, pxs, pys, prs, oxs, oys, obs) = take(7)
        ins = take(FIELDS)
        rin, cin, kin = take(nxr), take(nyr), take(nxr * nyr)
        smooth_out, frac_out, mat_out = take(3)
        (wide, zone_mid, colbuf, cornerbuf, rowzone) = take(5)
        (rm, cx, cy, count, seen, frac, fluxx, fluxy, moved, px_, py_, gs_, grad, grad2) = take(14)
        (mid_sem, row_sem, col_sem, corner_sem) = take(4)
        res, shp, rs = wide.at[0], wide.at[1], wide.at[2]
        mat, adj, adm = wide.at[4], wide.at[5], wide.at[6]

        tx, ty = lax.axis_index("tx"), lax.axis_index("ty")
        copies = []
        for f in range(FIELDS):
            into = (
                zone_mid
                if f == 2
                else (frac.at[0] if f == 3 else wide.at[f]).at[pl.ds(EDGE, tile_rows), pl.ds(0, tile_cols)]
            )
            copies.append(pltpu.make_async_copy(ins[f], into, mid_sem.at[f]))
        for j in range(nyr):
            copies.append(pltpu.make_async_copy(cin[j], colbuf.at[j], col_sem.at[j]))
        for i in range(nxr * nyr):
            copies.append(pltpu.make_async_copy(kin[i], cornerbuf.at[i], corner_sem.at[i]))
        tops = []
        for i, px in enumerate(xr):
            to = jnp.where(forward_of("tx", px), tile_rows + EDGE, 0)
            to = pl.multiple_of(to, EDGE)
            tops.append(to)
            for f in range(FIELDS):
                target = frac.at[0] if f == 3 else wide.at[f]
                copies.append(
                    pltpu.make_async_copy(
                        rin[i].at[pl.ds(EDGE * f, EDGE)],
                        target.at[pl.ds(to, EDGE), pl.ds(0, tile_cols)],
                        row_sem.at[i, f],
                    )
                )
        if nxr < 2:
            for f in range(FIELDS):
                target = frac.at[0] if f == 3 else wide.at[f]
                target[0:EDGE, :] = jnp.zeros((EDGE, cols), f32)
                target[rows - EDGE : rows, :] = jnp.zeros((EDGE, cols), f32)
        for copy in copies:
            copy.start()

        lane = lane_iota(EDGE, cols)
        col = jnp.where(lane < tile_cols + LANES // 2, lane, lane - cols)
        gcol = col + ty * tile_cols
        total_cols, total_rows = tile_cols * ny, tile_rows * nx
        col_in_grid = (gcol >= 0) & (gcol < total_cols)
        col_face = (gcol >= 0) & (gcol + 1 < total_cols)
        sub = lax.broadcasted_iota(jnp.int32, (EDGE, cols), 0)
        row0 = tx * tile_rows - EDGE

        zero = jnp.zeros((EDGE, cols), f32)

        def clear(k, carry):
            at = pl.ds(pl.multiple_of(k * EDGE, EDGE), EDGE)
            count[at, :] = zero
            for n in range(steps):
                seen[n, at, :] = zero
            return carry

        lax.fori_loop(0, chunks, clear, 0, unroll=2)
        one_lane = lane_iota(1, cols)

        def place(gx, gy):
            lr = gx - row0
            lc = gy - ty * tile_cols
            ok = (lr >= 0) & (lr < rows) & (lc >= -EDGE) & (lc < tile_cols + EDGE)
            return lr, jnp.where(lc < 0, lc + cols, lc), ok

        def well(o, carry):
            lr, ll, ok = place(oxs[o], oys[o])

            @pl.when(ok)
            def _():
                hit = one_lane == ll
                at = pl.ds(lr, 1)
                count[at, :] += jnp.where(hit, 1.0, 0.0)
                for n in range(steps):
                    seen[n, at, :] += jnp.where(hit, obs[n, o], 0.0)

            return carry

        lax.fori_loop(0, wells, well, 0)

        for copy in copies:
            copy.wait()

        def widen(k, carry):
            at = pl.ds(pl.multiple_of((k + 1) * EDGE, EDGE), EDGE)
            wide[2, at, 0:tile_cols] = zone_mid[pl.ds(pl.multiple_of(k * EDGE, EDGE), EDGE), :].astype(f32)
            return carry

        lax.fori_loop(0, tile_rows // EDGE, widen, 0, unroll=tile_rows // EDGE)
        edge_lane = lane_iota(EDGE, LANES)
        side = []
        for py in yr:
            ahead = forward_of("ty", py)
            low = jnp.where(ahead, 0, LANES - EDGE)
            side.append((edge_lane >= low) & (edge_lane < low + EDGE))

        def edge_of(messages, amount):
            out = jnp.zeros((EDGE, LANES), f32)
            for mask, message in zip(side, messages):
                part = pltpu.roll(message, (LANES - amount) % LANES, 1) if amount % LANES else message
                out = jnp.where(mask, part, out)
            return out

        def put_edge(f, at, value):
            target = frac.at[0] if f == 3 else wide.at[f]
            target[at, tile_cols:cols] = value

        for h in range(2):

            def fringe(k, carry):
                src = pl.ds(pl.multiple_of(k * EDGE, EDGE), EDGE)
                at = pl.ds(pl.multiple_of(k * EDGE + EDGE + h * half, EDGE), EDGE)
                messages = [colbuf[j, src, :] for j in range(nyr)]
                for f in range(FIELDS):
                    put_edge(f, at, edge_of(messages, EDGE * f + 64 * h))
                return carry

            lax.fori_loop(0, half // EDGE, fringe, 0, unroll=half // EDGE)
        for i in range(nxr):
            messages = [cornerbuf[i * nyr + j] for j in range(nyr)]
            for f in range(FIELDS):
                put_edge(f, pl.ds(tops[i], EDGE), edge_of(messages, EDGE * f))

        def at_of(k):
            return pl.ds(pl.multiple_of(k * EDGE, EDGE), EDGE)

        def next_of(k):
            return at_of(jnp.minimum(k + 1, chunks - 1))

        def up1(x):
            return pltpu.roll(x, EDGE - 1, 0)

        def down1(x):
            return pltpu.roll(x, 1, 0)

        def right(x):
            return pltpu.roll(x, cols - 1, 1)

        def left(x):
            return pltpu.roll(x, 1, 1)

        last, first = sub == EDGE - 1, sub == 0
        inv_f = [1.0 / jnp.full((EDGE, cols), st[0, z], f32) for z in range(zones)]
        inv_m = [1.0 / jnp.full((EDGE, cols), st[1, z], f32) for z in range(zones)]

        def prepare(k, carry):
            at = at_of(k)
            res[at, :] = jnp.exp(-res[at, :])
            shp[at, :] = jnp.exp(shp[at, :])
            zone = rs[at, :]
            a, b = inv_f[0], inv_m[0]
            for z in range(1, zones):
                hit = zone == float(z)
                a = jnp.where(hit, inv_f[z], a)
                b = jnp.where(hit, inv_m[z], b)
            rs[at, :] = a
            rm[at, :] = b
            return carry

        lax.fori_loop(0, chunks, prepare, 0, unroll=42)

        def links(k, carry):
            at = at_of(k)
            here = res[at, :]
            below = jnp.where(last, up1(res[next_of(k), :]), up1(here))
            beside = right(here)
            grow = row0 + k * EDGE + sub
            ok = (grow >= 0) & (grow + 1 < total_rows)
            cx[at, :] = jnp.where(ok, 2.0 / (here + below), 0.0)
            cy[at, :] = jnp.where(col_face, 2.0 / (here + beside), 0.0)
            return carry

        lax.fori_loop(0, chunks, links, 0, unroll=42)

        for n in range(steps):
            src, dst = frac.at[n], frac.at[n + 1]

            def step(k, carry, src=src, dst=dst, n=n):
                f, fup, flux_above = carry
                at = at_of(k)
                f_next = src[next_of(k), :]
                fup_next = up1(f_next)
                m = mat[at, :]
                fx = cx[at, :] * (jnp.where(last, fup_next, fup) - f)
                fy = cy[at, :] * (right(f) - f)
                fx_down = down1(fx)
                flow = fx - jnp.where(first, flux_above, fx_down) + fy - left(fy)
                t = shp[at, :] * (f - m)
                dst[at, :] = f + (flow - t) * rs[at, :]
                mat[at, :] = m + t * rm[at, :]
                fluxx[n, at, :] = fx
                fluxy[n, at, :] = fy
                moved[n, at, :] = t
                return f_next, fup_next, fx_down

            f0 = src[0:EDGE, :]
            lax.fori_loop(0, chunks, step, (f0, up1(f0), zero), unroll=42)
            for p in range(pumps):
                lr, ll, ok = place(pxs[0, p], pys[0, p])

                @pl.when(ok)
                def _(lr=lr, ll=ll, p=p, n=n, dst=dst):
                    at = pl.ds(lr, 1)
                    dst[at, :] += jnp.where(one_lane == ll, prs[n, p], 0.0) * rs[at, :]

        for n in reversed(range(steps)):
            opening, closing = n == steps - 1, n == 0

            def load(at, n=n):
                a = adj[at, :] + (count[at, :] * frac[n + 1, at, :] - seen[n, at, :])
                return a, a * rs[at, :]

            def back(k, carry, n=n, opening=opening, closing=closing, load=load):
                a, s, sup, flux_above, prod_above = carry
                at = at_of(k)
                a_next, s_next = load(next_of(k))
                sup_next = up1(s_next)
                sx = cx[at, :] * (jnp.where(last, sup_next, sup) - s)
                sy = cy[at, :] * (right(s) - s)
                sx_down = down1(sx)
                flow = sx - jnp.where(first, flux_above, sx_down) + sy - left(sy)
                am = adm[at, :]
                q = am * rm[at, :] - s
                swap = shp[at, :] * q
                gx = fluxx[n, at, :] * sx
                gy = fluxy[n, at, :] * sy
                gs = moved[n, at, :] * q
                if not opening:
                    gx += px_[at, :]
                    gy += py_[at, :]
                    gs += gs_[at, :]
                a_new = a + flow + swap
                am_new = am - swap
                adj[at, :] = a_new
                adm[at, :] = am_new
                if closing:
                    gx_down = down1(gx)
                    total = gx + jnp.where(first, prod_above, gx_down) + gy + left(gy)
                    grow = row0 + k * EDGE + sub
                    inside = (grow >= 0) & (grow < total_rows) & col_in_grid
                    grad[0, at, :] = jnp.where(inside, -0.5 * res[at, :] * total, 0.0)
                    grad[1, at, :] = jnp.where(inside, gs, 0.0)
                else:
                    gx_down = prod_above
                    px_[at, :] = gx
                    py_[at, :] = gy
                    gs_[at, :] = gs
                return a_next, s_next, sup_next, sx_down, gx_down

            a0, s0 = load(pl.ds(0, EDGE))
            lax.fori_loop(0, chunks, back, (a0, s0, up1(s0), zero, zero), unroll=42)

        out_copies = [
            pltpu.make_async_copy(
                adj.at[pl.ds(EDGE, tile_rows), pl.ds(0, tile_cols)], frac_out, mid_sem.at[0]
            ),
            pltpu.make_async_copy(
                adm.at[pl.ds(EDGE, tile_rows), pl.ds(0, tile_cols)], mat_out, mid_sem.at[1]
            ),
        ]
        for copy in out_copies:
            copy.start()

        def blur(source, q, k, g, gup, above):
            g_next = source[q, next_of(k), :]
            gup_next = up1(g_next)
            g_down = down1(g)
            around = jnp.where(last, gup_next, gup) + jnp.where(first, above, g_down)
            around = around + left(g) + right(g)
            return g + BLEND * (around - 4.0 * g), (g_next, gup_next, g_down)

        for q in range(2):

            def first_pass(k, carry, q=q):
                value, carry = blur(grad, q, k, *carry)
                grow = row0 + k * EDGE + sub
                inside = (grow >= 0) & (grow < total_rows) & col_in_grid
                grad2[q, at_of(k), :] = jnp.where(inside, value, 0.0)
                return carry

            g0 = grad[q, 0:EDGE, :]
            lax.fori_loop(0, chunks, first_pass, (g0, up1(g0), zero), unroll=42)

            def second_pass(k, carry, q=q):
                value, carry = blur(grad2, q, k, *carry)
                at = pl.ds(pl.multiple_of((k - 1) * EDGE, EDGE), EDGE)
                smooth_out[q, at, :] = value[:, 0:tile_cols]
                return carry

            g0 = grad2[q, EDGE : 2 * EDGE, :]
            lax.fori_loop(
                1,
                chunks - 1,
                second_pass,
                (g0, up1(g0), down1(grad2[q, 0:EDGE, :])),
                unroll=40,
            )
        for copy in out_copies:
            copy.wait()

    smem = pl.BlockSpec(memory_space=pltpu.SMEM)
    hbm = pl.BlockSpec(memory_space=pl.ANY)
    big = (rows, cols)
    return pl.pallas_call(
        kernel,
        out_shape=[
            jax.ShapeDtypeStruct((2, tile_rows, tile_cols), f32),
            jax.ShapeDtypeStruct((tile_rows, tile_cols), f32),
            jax.ShapeDtypeStruct((tile_rows, tile_cols), f32),
        ],
        in_specs=[smem] * 7 + [hbm] * (FIELDS + nxr + nyr + nxr * nyr),
        out_specs=[pl.BlockSpec(memory_space=pltpu.VMEM), hbm, hbm],
        scratch_shapes=[
            pltpu.VMEM((FIELDS,) + big, f32),
            pltpu.VMEM((tile_rows, tile_cols), jnp.int32),
            pltpu.VMEM((max(nyr, 1), half, LANES), f32),
            pltpu.VMEM((max(nxr * nyr, 1), EDGE, LANES), f32),
            pltpu.VMEM((EDGE, LANES), f32),
            pltpu.VMEM(big, f32),
            pltpu.VMEM(big, f32),
            pltpu.VMEM(big, f32),
            pltpu.VMEM(big, f32),
            pltpu.VMEM((steps,) + big, f32),
            pltpu.VMEM((steps + 1,) + big, f32),
            pltpu.VMEM((steps,) + big, f32),
            pltpu.VMEM((steps,) + big, f32),
            pltpu.VMEM((steps,) + big, f32),
            pltpu.VMEM(big, f32),
            pltpu.VMEM(big, f32),
            pltpu.VMEM(big, f32),
            pltpu.VMEM((2,) + big, f32),
            pltpu.VMEM((2,) + big, f32),
            pltpu.SemaphoreType.DMA((FIELDS,)),
            pltpu.SemaphoreType.DMA((nxr, FIELDS)),
            pltpu.SemaphoreType.DMA((max(nyr, 1),)),
            pltpu.SemaphoreType.DMA((max(nxr * nyr, 1),)),
        ],
        name="window",
    )(*scalars, *fields, *row_in, *col_in, *corner_in)


def on_device(
    log_cond,
    log_shape,
    zone_ids,
    storage,
    pump_x,
    pump_y,
    pump_rates,
    obs_x,
    obs_y,
    observed,
    frac_start,
    matrix_start,
    frac_end,
    matrix_end,
):
    nx, ny = lax.axis_size("tx"), lax.axis_size("ty")
    xr, yr = rounds_of(nx), rounds_of(ny)
    fields = (
        log_cond,
        log_shape,
        zone_ids,
        frac_start[0],
        matrix_start[0],
        frac_end[0],
        matrix_end[0],
    )
    row_out, col_out, corner_out = pack(fields, xr, yr)
    col_in = [lax.ppermute(m, "ty", pairs_of(ny, py)) for m, py in zip(col_out, yr)]
    row_in = [lax.ppermute(m, "tx", pairs_of(nx, px)) for m, px in zip(row_out, xr)]
    corner_in = [
        lax.ppermute(corner_out[i * len(yr) + j], ("tx", "ty"), corner_pairs(nx, ny, px, py))
        for i, px in enumerate(xr)
        for j, py in enumerate(yr)
    ]
    scalars = (storage, pump_x, pump_y, pump_rates[0], obs_x, obs_y, observed[0])
    smoothed, fracture_adj, matrix_adj = window(
        fields, scalars, row_in, col_in, corner_in, xr, yr, nx, ny
    )
    tests = lax.axis_size("test")
    summed = smoothed
    if tests == 2:
        summed = smoothed + lax.ppermute(smoothed, "test", [(0, 1), (1, 0)])
    else:
        summed = lax.psum(smoothed, "test")
    return (summed[0], summed[1], fracture_adj[None], matrix_adj[None])


def solution(mesh):
    placed = (
        P(("inv", "tx"), "ty"),
        P(("inv", "tx"), "ty"),
        P(("inv", "tx"), "ty"),
        P("inv", None),
        P(("inv", "test"), None),
        P(("inv", "test"), None),
        P(("inv", "test"), None, None),
        P("inv"),
        P("inv"),
        P(("inv", "test"), None, None),
        P(("inv", "test"), "tx", "ty"),
        P(("inv", "test"), "tx", "ty"),
        P(("inv", "test"), "tx", "ty"),
        P(("inv", "test"), "tx", "ty"),
    )
    return jax.shard_map(
        on_device,
        mesh=mesh,
        in_specs=placed,
        out_specs=(
            P(("inv", "tx"), "ty"),
            P(("inv", "tx"), "ty"),
            P(("inv", "test"), "tx", "ty"),
            P(("inv", "test"), "tx", "ty"),
        ),
        check_vma=False,
    )
```

```python
import jax
import jax.numpy as jnp
from jax import lax
from jax.experimental import pallas as pl
from jax.experimental.pallas import tpu as pltpu
from jax.sharding import PartitionSpec as P

SMOOTH = 2
EDGE = 8
LANES = 128
BLEND = 0.2
LEAD = 6
LAG = 6
FIELDS = 7


def in_vmem(x):
    return pltpu.with_memory_space_constraint(x, pltpu.VMEM)


def pairs_of(count, parity):
    found = []
    for low in range(parity, count - 1, 2):
        found += [(low, low + 1), (low + 1, low)]
    return found


def rounds_of(count):
    return [parity for parity in (0, 1) if pairs_of(count, parity)]


def partner(index, parity):
    return index + 1 if index % 2 == parity else index - 1


def corner_pairs(nx, ny, px, py):
    found = []
    for x in range(nx):
        for y in range(ny):
            there = (partner(x, px), partner(y, py))
            if 0 <= there[0] < nx and 0 <= there[1] < ny:
                found.append((x * ny + y, there[0] * ny + there[1]))
    return found


def forward_of(axis, parity):
    return lax.rem(lax.axis_index(axis), 2) == parity


def lane_iota(rows, cols):
    return lax.broadcasted_iota(jnp.int32, (rows, cols), 1)


def pack(fields, xr, yr):
    tile_rows, tile_cols = fields[0].shape
    half = tile_rows // 2
    nxr, nyr = len(xr), len(yr)

    def kernel(*refs):
        ins = refs[:FIELDS]
        row_out = refs[FIELDS : FIELDS + nxr]
        col_out = refs[FIELDS + nxr : FIELDS + nxr + nyr]
        corner_out = refs[FIELDS + nxr + nyr : FIELDS + nxr + nyr + nxr * nyr]
        rest = refs[FIELDS + nxr + nyr + nxr * nyr :]
        zone_rows, cols, zone_cols, row_sem, col_sem = rest
        row_copies = []
        for i, px in enumerate(xr):
            start = jnp.where(forward_of("tx", px), tile_rows - EDGE, 0)
            start = pl.multiple_of(start, EDGE)
            for f in range(FIELDS):
                into = zone_rows.at[i] if f == 2 else row_out[i].at[pl.ds(EDGE * f, EDGE)]
                row_copies.append(
                    pltpu.make_async_copy(
                        ins[f].at[pl.ds(start, EDGE)], into, row_sem.at[i, f]
                    )
                )
        col_copies = []
        for j, py in enumerate(yr):
            start = jnp.where(forward_of("ty", py), tile_cols - LANES, 0)
            start = pl.multiple_of(start, LANES)
            for f in range(FIELDS):
                into = zone_cols.at[j] if f == 2 else cols.at[j, f]
                col_copies.append(
                    pltpu.make_async_copy(
                        ins[f].at[:, pl.ds(start, LANES)], into, col_sem.at[j, f]
                    )
                )
        for copy in row_copies + col_copies:
            copy.start()
        for copy in row_copies:
            copy.wait()
        for i in range(nxr):
            row_out[i][2 * EDGE : 3 * EDGE, :] = zone_rows[i].astype(jnp.float32)
        slot = lane_iota(EDGE, LANES) // EDGE
        for i in range(nxr):
            for j, py in enumerate(yr):
                ahead = forward_of("ty", py)
                shift = jnp.where(ahead, 1, 0)
                total = jnp.zeros((EDGE, LANES), jnp.float32)
                for f in range(FIELDS):
                    rows = row_out[i][EDGE * f : EDGE * (f + 1), :]
                    part = jnp.where(ahead, rows[:, tile_cols - LANES :], rows[:, :LANES])
                    part = pltpu.roll(part, EDGE * f, 1)
                    want = lax.rem(f - shift + 16, 16)
                    total = jnp.where(slot == want, part, total)
                corner_out[i * nyr + j][...] = total
        for copy in col_copies:
            copy.wait()
        for j, py in enumerate(yr):
            shift = jnp.where(forward_of("ty", py), 1, 0)

            def body(k, carry):
                total = jnp.zeros((EDGE, LANES), jnp.float32)
                for h in range(2):
                    at = pl.multiple_of(k * EDGE + h * half, EDGE)
                    for f in range(FIELDS):
                        if f == 2:
                            part = zone_cols[j, pl.ds(at, EDGE), :].astype(jnp.float32)
                        else:
                            part = cols[j, f, pl.ds(at, EDGE), :]
                        amount = EDGE * f + 64 * h
                        part = pltpu.roll(part, amount, 1) if amount else part
                        want = lax.rem(f + 8 * h - shift + 16, 16)
                        total = jnp.where(slot == want, part, total)
                col_out[j][pl.ds(pl.multiple_of(k * EDGE, EDGE), EDGE), :] = total
                return carry

            lax.fori_loop(0, half // EDGE, body, 0, unroll=half // EDGE)

    outs = [pltpu.VMEM((EDGE * FIELDS, tile_cols), jnp.float32)] * nxr
    outs += [pltpu.VMEM((half, LANES), jnp.float32)] * nyr
    outs += [pltpu.VMEM((EDGE, LANES), jnp.float32)] * (nxr * nyr)
    made = pl.pallas_call(
        kernel,
        out_shape=outs,
        in_specs=[pl.BlockSpec(memory_space=pltpu.HBM)] * FIELDS,
        out_specs=[pl.BlockSpec(memory_space=pltpu.VMEM)] * len(outs),
        scratch_shapes=[
            pltpu.VMEM((nxr, EDGE, tile_cols), jnp.int32),
            pltpu.VMEM((nyr, FIELDS, tile_rows, LANES), jnp.float32),
            pltpu.VMEM((nyr, tile_rows, LANES), jnp.int32),
            pltpu.SemaphoreType.DMA((nxr, FIELDS)),
            pltpu.SemaphoreType.DMA((nyr, FIELDS)),
        ],
        name="pack",
    )(*fields)
    return made[:nxr], made[nxr : nxr + nyr], made[nxr + nyr :]


def window(fields, scalars, row_in, col_in, corner_in, xr, yr, nx, ny):
    tile_rows, tile_cols = fields[0].shape
    storage, pump_rates, spots, observed = scalars
    zones = storage.shape[1]
    pumps, steps = pump_rates.shape
    wells = observed.shape[2]
    assert 2 * steps + SMOOTH <= EDGE
    half = tile_rows // 2
    nxr, nyr = len(xr), len(yr)
    rows = tile_rows + 2 * EDGE
    chunks = rows // EDGE
    own = tile_cols // LANES
    tiles = own + 1
    f32 = jnp.float32

    def kernel(*refs):
        pos = 0

        def take(count):
            nonlocal pos
            pos += count
            return refs[pos - count : pos]

        small_in = take(4)
        ins = take(FIELDS)
        rin, cin, kin = take(nxr), take(nyr), take(nxr * nyr)
        smooth_out, frac_out, mat_out = take(3)
        (wide, zone_mid) = take(2)
        (rm, cx, cy, count, seen, frac, fluxx, fluxy, moved, scaled, flux, prod) = take(12)
        (px_, py_, gs_, grad, grad2) = take(5)
        (st, prs, spot, obs) = take(4)
        (mid_sem, small_sem) = take(2)
        res, shp, rs = wide.at[0], wide.at[1], wide.at[2]
        mat, adj, adm = wide.at[4], wide.at[5], wide.at[6]
        tx, ty = lax.axis_index("tx"), lax.axis_index("ty")

        def field(f):
            return frac.at[0] if f == 3 else wide.at[f]

        def at_of(k, shift=0):
            return slice(EDGE * (k + 1) + shift, EDGE * (k + 2) + shift)

        def get(ref, k, shift=0):
            return ref[:, at_of(k, shift), :]

        def put(ref, k, value):
            ref[:, at_of(k), :] = value

        small = [
            pltpu.make_async_copy(a, b, small_sem.at[i])
            for i, (a, b) in enumerate(zip(small_in, (st, prs, spot, obs)))
        ]
        copies = []
        for f in range(FIELDS):
            for t in range(own):
                into = zone_mid.at[t] if f == 2 else field(f).at[t, pl.ds(2 * EDGE, tile_rows)]
                copies.append(
                    pltpu.make_async_copy(
                        ins[f].at[:, pl.ds(LANES * t, LANES)], into, mid_sem.at[f, t]
                    )
                )
        tops = []
        for i, px in enumerate(xr):
            to = jnp.where(forward_of("tx", px), tile_rows + 2 * EDGE, EDGE)
            to = pl.multiple_of(to, EDGE)
            tops.append(to)
        block = (tiles, EDGE, LANES)
        zero = jnp.zeros(block, f32)
        if nxr < 2:
            for f in range(FIELDS):
                put(field(f), 0, zero)
                put(field(f), chunks - 1, zero)
        for copy in small + copies:
            copy.start()
        for ref in (
            [res, grad.at[0], grad.at[1], grad2.at[0], grad2.at[1], flux, prod]
            + [frac.at[n] for n in range(steps + 1)]
            + [fluxx.at[n] for n in range(steps)]
            + [scaled.at[n] for n in range(2)]
        ):
            put(ref, -1, zero)
            put(ref, chunks, zero)

        def iota(axis):
            return lax.broadcasted_iota(jnp.int32, block, axis)

        lane = iota(2)
        where_col = iota(0) * LANES + lane
        col = jnp.where(where_col < tile_cols + LANES // 2, where_col, where_col - tiles * LANES)
        gcol = col + ty * tile_cols
        total_cols, total_rows = tile_cols * ny, tile_rows * nx
        col_in_grid = (gcol >= 0) & (gcol < total_cols)
        col_face = (gcol >= 0) & (gcol + 1 < total_cols)
        row0 = tx * tile_rows - EDGE
        sub = iota(1)
        last_lane, first_lane = lane == LANES - 1, lane == 0

        def right(x):
            turned = pltpu.roll(x, LANES - 1, 2)
            beside = jnp.concatenate([turned[1:], turned[:1]], 0)
            return jnp.where(last_lane, beside, turned)

        def left(x):
            turned = pltpu.roll(x, 1, 2)
            beside = jnp.concatenate([turned[-1:], turned[:-1]], 0)
            return jnp.where(first_lane, beside, turned)

        for k in range(chunks):
            put(count, k, zero)
            for n in range(steps):
                put(seen.at[n], k, zero)
        one_lane = lane_iota(1, LANES)
        for copy in small:
            copy.wait()

        def place(gx, gy):
            lr = gx - row0
            lc = gy - ty * tile_cols
            ok = (lr >= 0) & (lr < rows) & (lc >= -EDGE) & (lc < tile_cols + EDGE)
            at = jnp.where(lc < 0, lc + tiles * LANES, lc)
            return lr + EDGE, at // LANES, lax.rem(at, LANES), ok

        def well(o, carry):
            lr, lt, ll, ok = place(spot[2 * pumps + o], spot[2 * pumps + wells + o])

            @pl.when(ok)
            def _():
                hit = one_lane == ll
                at = pl.ds(lr, 1)
                count[lt, at, :] += jnp.where(hit, 1.0, 0.0)
                for n in range(steps):
                    seen[n, lt, at, :] += jnp.where(hit, obs[n, 0, o], 0.0)

            return carry

        lax.fori_loop(0, wells, well, 0)

        by_lane = lane_iota(EDGE, LANES)
        stores = []
        for kind in range(2):
            table = jnp.full((EDGE, LANES), st[kind, 0], f32)
            for z in range(1, zones):
                table = jnp.where(by_lane == z, st[kind, z], table)
            stores.append(1.0 / table)

        for copy in copies:
            copy.wait()
        for i in range(nxr):
            for f in range(FIELDS):
                for t in range(own):
                    field(f)[t, pl.ds(tops[i], EDGE), :] = rin[i][
                        EDGE * f : EDGE * (f + 1), LANES * t : LANES * (t + 1)
                    ]

        edge_lane = lane_iota(EDGE, LANES)
        side = []
        for py in yr:
            low = jnp.where(forward_of("ty", py), 0, LANES - EDGE)
            side.append((edge_lane >= low) & (edge_lane < low + EDGE))

        def edge_of(messages, amount):
            out = jnp.zeros((EDGE, LANES), f32)
            for mask, message in zip(side, messages):
                part = pltpu.roll(message, (LANES - amount) % LANES, 1) if amount % LANES else message
                out = jnp.where(mask, part, out)
            return out

        for h in range(2):
            for k in range(half // EDGE):
                messages = [cin[j][EDGE * k : EDGE * (k + 1), :] for j in range(nyr)]
                for f in range(FIELDS):
                    value = edge_of(messages, EDGE * f + 64 * h)
                    field(f)[own, at_of(k + 1 + h * (half // EDGE)), :] = value
        for i in range(nxr):
            messages = [kin[i * nyr + j][...] for j in range(nyr)]
            for f in range(FIELDS):
                field(f)[own, pl.ds(tops[i], EDGE), :] = edge_of(messages, EDGE * f)

        def inject(k, n):
            return get(count, k) * get(frac.at[n], k) - get(seen.at[n - 1], k)

        def look_up(table, index):
            return jnp.take_along_axis(table, index, axis=1, mode="promise_in_bounds")

        for k in range(chunks):
            put(res, k, jnp.exp(-get(res, k)))
            put(shp, k, jnp.exp(get(shp, k)))
            for t in range(tiles):
                if t < own and 0 < k < chunks - 1:
                    zone = zone_mid[t, EDGE * (k - 1) : EDGE * k, :]
                else:
                    zone = rs[t, at_of(k), :].astype(jnp.int32)
                rs[t, at_of(k), :] = look_up(stores[0], zone)
                rm[t, at_of(k), :] = look_up(stores[1], zone)

        def row_of(k):
            return row0 + k * EDGE + sub

        for k in range(chunks):
            here = get(res, k)
            down = 2.0 / (here + get(res, k, 1))
            if k in (0, chunks - 2, chunks - 1):
                down = jnp.where((row_of(k) >= 0) & (row_of(k) + 1 < total_rows), down, 0.0)
            put(cx, k, down)
            put(cy, k, jnp.where(col_face, 2.0 / (here + right(here)), 0.0))

        def in_grid(k, value):
            if k in (0, chunks - 1):
                keep = col_in_grid & (row_of(k) >= 0) & (row_of(k) < total_rows)
                return jnp.where(keep, value, 0.0)
            edge = jnp.where(col_in_grid[own:], value[own:], 0.0)
            return jnp.concatenate([value[:own], edge], 0)

        for n in range(steps):
            src, dst = frac.at[n], frac.at[n + 1]
            ahead, behind = {}, {}

            def update(k, src=src, dst=dst, n=n, behind=behind):
                fx, fy, fy_left, t = behind.pop(k)
                flow = fx - get(fluxx.at[n], k, -1) + (fy - fy_left)
                put(dst, k, get(src, k) + (flow - t) * get(rs, k))

            for k in range(chunks + LEAD):
                if k < chunks:
                    ahead[k] = right(get(src, k))
                if k >= LEAD:
                    j = k - LEAD
                    f, m = get(src, j), get(mat, j)
                    fx = get(cx, j) * (get(src, j, 1) - f)
                    put(fluxx.at[n], j, fx)
                    fy = get(cy, j) * (ahead.pop(j) - f)
                    put(fluxy.at[n], j, fy)
                    t = get(shp, j) * (f - m)
                    put(moved.at[n], j, t)
                    put(mat, j, m + t * get(rm, j))
                    behind[j] = (fx, fy, left(fy), t)
                    if j >= LAG:
                        update(j - LAG)
            for j in range(chunks - LAG, chunks):
                update(j)
            for p in range(pumps):
                lr, lt, ll, ok = place(spot[p], spot[pumps + p])

                @pl.when(ok)
                def _(lr=lr, lt=lt, ll=ll, p=p, n=n, dst=dst):
                    at = pl.ds(lr, 1)
                    dst[lt, at, :] += jnp.where(one_lane == ll, prs[p, n], 0.0) * rs[lt, at, :]

        for k in range(chunks):
            a = get(adj, k) + inject(k, steps)
            put(adj, k, a)
            put(scaled.at[steps % 2], k, a * get(rs, k))
        for n in reversed(range(steps)):
            old, new = scaled.at[(n + 1) % 2], scaled.at[n % 2]
            ahead, behind, ends = {}, {}, {}

            def update(k, n=n, new=new, behind=behind):
                sx, sy, sy_left, swap = behind.pop(k)
                a = get(adj, k) + (sx - get(flux, k, -1) + (sy - sy_left)) + swap
                if n > 0:
                    a = a + inject(k, n)
                    put(new, k, a * get(rs, k))
                put(adj, k, a)

            def close(k, ends=ends):
                gx, gy, gy_left = ends.pop(k)
                total = gx + get(prod, k, -1) + (gy + gy_left)
                gc = -0.5 * get(res, k) * total
                put(grad.at[0], k, in_grid(k, gc))

            for k in range(chunks + LEAD):
                if k < chunks:
                    ahead[k] = right(get(old, k))
                if k < LEAD:
                    continue
                j = k - LEAD
                s = get(old, j)
                sx = get(cx, j) * (get(old, j, 1) - s)
                put(flux, j, sx)
                sy = get(cy, j) * (ahead.pop(j) - s)
                am = get(adm, j)
                q = am * get(rm, j) - s
                swap = get(shp, j) * q
                put(adm, j, am - swap)
                gx = get(fluxx.at[n], j) * sx
                gy = get(fluxy.at[n], j) * sy
                gs = get(moved.at[n], j) * q
                if n < steps - 1:
                    gx += get(px_, j)
                    gy += get(py_, j)
                    gs += get(gs_, j)
                behind[j] = (sx, sy, left(sy), swap)
                if n > 0:
                    put(px_, j, gx)
                    put(py_, j, gy)
                    put(gs_, j, gs)
                else:
                    put(prod, j, gx)
                    ends[j] = (gx, gy, left(gy))
                    put(grad.at[1], j, in_grid(j, gs))
                if j >= LAG:
                    update(j - LAG)
                    if n == 0:
                        close(j - LAG)
            for j in range(chunks - LAG, chunks):
                update(j)
                if n == 0:
                    close(j)

        out_copies = []
        for q, (source, out) in enumerate(((adj, frac_out), (adm, mat_out))):
            for t in range(own):
                out_copies.append(
                    pltpu.make_async_copy(
                        source.at[t, pl.ds(2 * EDGE, tile_rows)],
                        out.at[:, pl.ds(LANES * t, LANES)],
                        mid_sem.at[q, t],
                    )
                )
        for copy in out_copies:
            copy.start()

        def blur(source, ks, emit):
            turned = {}
            for i in range(len(ks) + LEAD):
                if i < len(ks):
                    g = get(source, ks[i])
                    turned[i] = left(g) + right(g)
                if i >= LEAD:
                    k = ks[i - LEAD]
                    around = get(source, k, -1) + get(source, k, 1) + turned.pop(i - LEAD)
                    emit(k, (1.0 - 4.0 * BLEND) * get(source, k) + BLEND * around)

        for q in range(2):

            def first(k, value, q=q):
                put(grad2.at[q], k, in_grid(k, value))

            blur(grad.at[q], list(range(chunks)), first)
        for q in range(2):

            def second(k, value, q=q):
                for t in range(own):
                    smooth_out[q, EDGE * (k - 1) : EDGE * k, LANES * t : LANES * (t + 1)] = value[t]

            blur(grad2.at[q], list(range(1, chunks - 1)), second)
        for copy in out_copies:
            copy.wait()

    hbm = pl.BlockSpec(memory_space=pltpu.HBM)
    vmem = pl.BlockSpec(memory_space=pltpu.VMEM)
    big = (tiles, rows + 2 * EDGE, LANES)
    flat = jax.ShapeDtypeStruct((tile_rows, tile_cols), f32)
    return pl.pallas_call(
        kernel,
        out_shape=[pltpu.VMEM((2, tile_rows, tile_cols), f32), flat, flat],
        in_specs=[hbm] * (4 + FIELDS) + [vmem] * (nxr + nyr + nxr * nyr),
        out_specs=[vmem, hbm, hbm],
        scratch_shapes=[
            pltpu.VMEM((FIELDS,) + big, f32),
            pltpu.VMEM((own, tile_rows, LANES), jnp.int32),
            pltpu.VMEM(big, f32),
            pltpu.VMEM(big, f32),
            pltpu.VMEM(big, f32),
            pltpu.VMEM(big, f32),
            pltpu.VMEM((steps,) + big, f32),
            pltpu.VMEM((steps + 1,) + big, f32),
            pltpu.VMEM((steps,) + big, f32),
            pltpu.VMEM((steps,) + big, f32),
            pltpu.VMEM((steps,) + big, f32),
            pltpu.VMEM((2,) + big, f32),
            pltpu.VMEM(big, f32),
            pltpu.VMEM(big, f32),
            pltpu.VMEM(big, f32),
            pltpu.VMEM(big, f32),
            pltpu.VMEM(big, f32),
            pltpu.VMEM((2,) + big, f32),
            pltpu.VMEM((2,) + big, f32),
        ]
        + [pltpu.SMEM(x.shape, x.dtype) for x in scalars]
        + [
            pltpu.SemaphoreType.DMA((FIELDS, own)),
            pltpu.SemaphoreType.DMA((4,)),
        ],
        name="window",
    )(*scalars, *fields, *(in_vmem(x) for x in row_in + col_in + corner_in))


def add_parts(mine, theirs):
    def kernel(a_ref, b_ref, cond_ref, shape_ref):
        cond_ref[...] = a_ref[0] + b_ref[0]
        shape_ref[...] = a_ref[1] + b_ref[1]

    vmem = pl.BlockSpec(memory_space=pltpu.VMEM)
    flat = jax.ShapeDtypeStruct(mine.shape[1:], mine.dtype)
    return pl.pallas_call(
        kernel, out_shape=[flat] * 2, in_specs=[vmem] * 2, out_specs=[vmem] * 2, name="add_parts"
    )(in_vmem(mine), in_vmem(theirs))


def on_device(
    log_cond,
    log_shape,
    zone_ids,
    storage,
    pump_x,
    pump_y,
    pump_rates,
    obs_x,
    obs_y,
    observed,
    frac_start,
    matrix_start,
    frac_end,
    matrix_end,
):
    nx, ny = lax.axis_size("tx"), lax.axis_size("ty")
    xr, yr = rounds_of(nx), rounds_of(ny)
    fields = (
        log_cond,
        log_shape,
        zone_ids,
        frac_start[0],
        matrix_start[0],
        frac_end[0],
        matrix_end[0],
    )
    row_out, col_out, corner_out = pack(fields, xr, yr)
    col_in = [lax.ppermute(m, "ty", pairs_of(ny, py)) for m, py in zip(col_out, yr)]
    row_in = [lax.ppermute(m, "tx", pairs_of(nx, px)) for m, px in zip(row_out, xr)]
    corner_in = [
        lax.ppermute(corner_out[i * len(yr) + j], ("tx", "ty"), corner_pairs(nx, ny, px, py))
        for i, px in enumerate(xr)
        for j, py in enumerate(yr)
    ]
    rates = jnp.transpose(pump_rates, (0, 2, 1))[0]
    spots = jnp.concatenate([pump_x[0], pump_y[0], obs_x, obs_y])
    scalars = (storage, rates, spots, jnp.transpose(observed, (1, 0, 2)))
    part, fracture_adj, matrix_adj = window(
        fields, scalars, row_in, col_in, corner_in, xr, yr, nx, ny
    )
    tests = lax.axis_size("test")
    if tests == 2:
        cond_sum, shape_sum = add_parts(part, lax.ppermute(part, "test", [(0, 1), (1, 0)]))
    else:
        cond_sum, shape_sum = lax.psum(part, "test")
    return (cond_sum, shape_sum, fracture_adj[None], matrix_adj[None])


def solution(mesh):
    placed = (
        P(("inv", "tx"), "ty"),
        P(("inv", "tx"), "ty"),
        P(("inv", "tx"), "ty"),
        P("inv", None),
        P(("inv", "test"), None),
        P(("inv", "test"), None),
        P(("inv", "test"), None, None),
        P("inv"),
        P("inv"),
        P(("inv", "test"), None, None),
        P(("inv", "test"), "tx", "ty"),
        P(("inv", "test"), "tx", "ty"),
        P(("inv", "test"), "tx", "ty"),
        P(("inv", "test"), "tx", "ty"),
    )
    return jax.shard_map(
        on_device,
        mesh=mesh,
        in_specs=placed,
        out_specs=(
            P(("inv", "tx"), "ty"),
            P(("inv", "tx"), "ty"),
            P(("inv", "test"), "tx", "ty"),
            P(("inv", "test"), "tx", "ty"),
        ),
        check_vma=False,
    )
```

```python
import jax
import jax.numpy as jnp
from jax import lax
from jax.experimental import pallas as pl
from jax.experimental.pallas import tpu as pltpu
from jax.sharding import PartitionSpec as P


SMOOTH = 2
EDGE = 8
LANES = 128
BLEND = 0.2
LEAD = 6
LAG = 6
FIELDS = 7


def in_vmem(x):
    return pltpu.with_memory_space_constraint(x, pltpu.VMEM)


def in_hbm(x):
    return pltpu.with_memory_space_constraint(x, pltpu.HBM)


def pairs_of(count, parity):
    found = []
    for low in range(parity, count - 1, 2):
        found += [(low, low + 1), (low + 1, low)]
    return found


def rounds_of(count):
    return [parity for parity in (0, 1) if pairs_of(count, parity)]


def forward_of(axis, parity):
    return lax.rem(lax.axis_index(axis), 2) == parity


def lane_iota(rows, cols):
    return lax.broadcasted_iota(jnp.int32, (rows, cols), 1)


def tile_shape(fields):
    tile_rows, tile_cols = fields[0].shape
    return tile_rows, tile_cols, tile_cols // LANES


def vmem_like(shape, kind=jnp.float32):
    return pltpu.VMEM(shape, kind)


HBM = pl.BlockSpec(memory_space=pltpu.HBM)
VMEM = pl.BlockSpec(memory_space=pltpu.VMEM)


def pack_columns(fields, yr):
    tile_rows, tile_cols, _ = tile_shape(fields)
    half = tile_rows // 2
    nyr = len(yr)

    def kernel(*refs):
        ins, outs = refs[:FIELDS], refs[FIELDS : FIELDS + nyr]
        cols, zone_cols, sem = refs[FIELDS + nyr :]
        copies = []
        for j, py in enumerate(yr):
            start = jnp.where(forward_of("ty", py), tile_cols - LANES, 0)
            start = pl.multiple_of(start, LANES)
            for f in range(FIELDS):
                into = zone_cols.at[j] if f == 2 else cols.at[j, f]
                copies.append(
                    pltpu.make_async_copy(ins[f].at[:, pl.ds(start, LANES)], into, sem.at[j, f])
                )
        for copy in copies:
            copy.start()
        for copy in copies:
            copy.wait()
        slot = lane_iota(EDGE, LANES) // EDGE
        for j, py in enumerate(yr):
            shift = jnp.where(forward_of("ty", py), 1, 0)
            masks = {}
            for h in range(2):
                for f in range(FIELDS):
                    masks[h, f] = slot == lax.rem(f + 8 * h - shift + 16, 16)
            for k in range(half // EDGE):
                total = jnp.zeros((EDGE, LANES), jnp.float32)
                for h in range(2):
                    at = k * EDGE + h * half
                    for f in range(FIELDS):
                        part = (zone_cols if f == 2 else cols.at[:, f])[j, at : at + EDGE, :]
                        amount = EDGE * f + 64 * h
                        part = part.astype(jnp.float32)
                        part = pltpu.roll(part, amount, 1) if amount else part
                        total = jnp.where(masks[h, f], part, total)
                outs[j][EDGE * k : EDGE * (k + 1), :] = total

    return pl.pallas_call(
        kernel,
        out_shape=[vmem_like((half, LANES))] * nyr,
        in_specs=[HBM] * FIELDS,
        out_specs=[VMEM] * nyr,
        scratch_shapes=[
            pltpu.VMEM((nyr, FIELDS, tile_rows, LANES), jnp.float32),
            pltpu.VMEM((nyr, tile_rows, LANES), jnp.int32),
            pltpu.SemaphoreType.DMA((nyr, FIELDS)),
        ],
        compiler_params=grant(8),
        name="pack_columns",
    )(*(in_hbm(x) for x in fields))


def load_tile(fields, xr):
    tile_rows, tile_cols, own = tile_shape(fields)
    nxr = len(xr)

    def kernel(*refs):
        ins = refs[:FIELDS]
        wide, zone_mid = refs[FIELDS : FIELDS + 2]
        outs = refs[FIELDS + 2 : FIELDS + 2 + nxr]
        sem = refs[FIELDS + 2 + nxr]
        copies = []
        for f in range(FIELDS):
            for t in range(own):
                into = zone_mid.at[t] if f == 2 else wide.at[f, t, pl.ds(2 * EDGE, tile_rows)]
                copies.append(
                    pltpu.make_async_copy(ins[f].at[:, pl.ds(LANES * t, LANES)], into, sem.at[f, t])
                )
        for copy in copies:
            copy.start()
        for copy in copies:
            copy.wait()
        for i, px in enumerate(xr):
            start = pl.multiple_of(jnp.where(forward_of("tx", px), tile_rows - EDGE, 0), EDGE)
            for f in range(FIELDS):
                for t in range(own):
                    if f == 2:
                        part = zone_mid[t, pl.ds(start, EDGE), :].astype(jnp.float32)
                    else:
                        part = wide[f, t, pl.ds(start + 2 * EDGE, EDGE), :]
                    outs[i][EDGE * f : EDGE * (f + 1), LANES * t : LANES * (t + 1)] = part

    big = (own + 1, tile_rows + 4 * EDGE, LANES)
    made = pl.pallas_call(
        kernel,
        out_shape=[
            vmem_like((FIELDS,) + big),
            vmem_like((own, tile_rows, LANES), jnp.int32),
        ]
        + [vmem_like((EDGE * (FIELDS + 1), tile_cols))] * nxr,
        in_specs=[HBM] * FIELDS,
        out_specs=[VMEM] * (2 + nxr),
        scratch_shapes=[pltpu.SemaphoreType.DMA((FIELDS, own))],
        compiler_params=grant(4),
        name="load_tile",
    )(*(in_hbm(x) for x in fields))
    return made[0], made[1], made[2:]


def add_corners(row_out, col_in, xr):
    nxr, nyr = len(xr), len(col_in)
    assert nyr * LANES <= row_out[0].shape[1]

    def kernel(*refs):
        cols, outs = refs[:nyr], refs[nyr + nxr :]
        for i, px in enumerate(xr):
            outs[i][EDGE * FIELDS :, :] = jnp.zeros((EDGE, row_out[0].shape[1]), jnp.float32)
            ahead = forward_of("tx", px)
            for j in range(nyr):
                top = cols[j][0:EDGE, :]
                low = pltpu.roll(cols[j][cols[j].shape[0] - EDGE :, :], LANES // 2, 1)
                outs[i][EDGE * FIELDS :, LANES * j : LANES * (j + 1)] = jnp.where(ahead, low, top)

    return pl.pallas_call(
        kernel,
        out_shape=[vmem_like(x.shape) for x in row_out],
        in_specs=[VMEM] * (nyr + nxr),
        out_specs=[VMEM] * nxr,
        input_output_aliases={nyr + i: i for i in range(nxr)},
        compiler_params=grant(2),
        name="add_corners",
    )(*(in_vmem(x) for x in list(col_in) + list(row_out)))


def grant(mib):
    return pltpu.CompilerParams(vmem_limit_bytes=mib * 2**20)


class Chunks:
    def __init__(self, tile_rows):
        self.count = tile_rows // EDGE + 2

    @staticmethod
    def at(k, shift=0):
        return slice(EDGE * (k + 1) + shift, EDGE * (k + 2) + shift)


def get(ref, k, shift=0):
    return ref[:, Chunks.at(k, shift), :]


def put(ref, k, value):
    ref[:, Chunks.at(k), :] = value


def turn_right(x, last_lane):
    turned = pltpu.roll(x, LANES - 1, 2)
    return jnp.where(last_lane, jnp.concatenate([turned[1:], turned[:1]], 0), turned)


def turn_left(x, first_lane):
    turned = pltpu.roll(x, 1, 2)
    return jnp.where(first_lane, jnp.concatenate([turned[-1:], turned[:-1]], 0), turned)


def store_tables(storage_ref, zones):
    by_lane = lane_iota(EDGE, LANES)
    tables = []
    for kind in range(2):
        table = jnp.full((EDGE, LANES), storage_ref[kind, 0], jnp.float32)
        for z in range(1, zones):
            table = jnp.where(by_lane == z, storage_ref[kind, z], table)
        tables.append(1.0 / table)
    return tables


def look_up(table, index):
    return jnp.take_along_axis(table, index, axis=1, mode="promise_in_bounds")


def place_of(gx, gy, tile_rows, tile_cols):
    lr = gx - lax.axis_index("tx") * tile_rows + EDGE
    lc = gy - lax.axis_index("ty") * tile_cols
    ok = (lr >= 0) & (lr < tile_rows + 2 * EDGE) & (lc >= -EDGE) & (lc < tile_cols + EDGE)
    at = jnp.where(lc < 0, lc + tile_cols + LANES, lc)
    return lr + EDGE, at // LANES, lax.rem(at, LANES), ok


def prepare_tile(wide, zone_mid, scalars):
    storage, _, _, observed = scalars
    tile_rows = zone_mid.shape[1]
    own = zone_mid.shape[0]
    tile_cols = own * LANES
    big = wide.shape[1:]
    zones = storage.shape[1]
    steps, wells = observed.shape[0], observed.shape[2]
    chunks = Chunks(tile_rows).count
    f32 = jnp.float32

    def kernel(*refs):
        small_in, zone_in = refs[:4], refs[5]
        wide, rm, cx, cy, count, seen = refs[6:12]
        st, oxs, oys, obs = refs[12:16]
        sem = refs[16]
        copies = [
            pltpu.make_async_copy(a, b, sem.at[i])
            for i, (a, b) in enumerate(zip(small_in, (st, oxs, oys, obs)))
        ]
        for copy in copies:
            copy.start()
        res, shp, rs = wide.at[0], wide.at[1], wide.at[2]
        zero = jnp.zeros((own + 1, EDGE, LANES), f32)
        for k in range(chunks):
            put(count, k, zero)
            for n in range(steps):
                put(seen.at[n], k, zero)
        for k in range(1, chunks - 1):
            res[0:own, Chunks.at(k), :] = jnp.exp(-res[0:own, Chunks.at(k), :])
            shp[0:own, Chunks.at(k), :] = jnp.exp(shp[0:own, Chunks.at(k), :])
        last_lane = lax.broadcasted_iota(jnp.int32, (1, EDGE, LANES), 2) == LANES - 1
        ahead = {}
        for k in range(1, chunks - 1 + LEAD):
            if k < chunks - 1:
                turned = pltpu.roll(res[0:own, Chunks.at(k), :], LANES - 1, 2)
                ahead[k] = jnp.where(last_lane, turned[1:], turned[:-1])
            j = k - LEAD
            if j >= 1:
                here = res[0:own, Chunks.at(j), :]
                if j < chunks - 2:
                    below = res[0:own, Chunks.at(j, 1), :]
                    cx[0:own, Chunks.at(j), :] = 2.0 / (here + below)
                cy[0 : own - 1, Chunks.at(j), :] = 2.0 / (here[: own - 1] + ahead.pop(j))
        for copy in copies:
            copy.wait()
        tables = store_tables(st, zones)
        for k in range(1, chunks - 1):
            for t in range(own):
                zone = zone_in[t, EDGE * (k - 1) : EDGE * k, :]
                rs[t, Chunks.at(k), :] = look_up(tables[0], zone)
                rm[t, Chunks.at(k), :] = look_up(tables[1], zone)
        one_lane = lane_iota(1, LANES)

        def well(o, carry):
            lr, lt, ll, ok = place_of(oxs[o], oys[o], tile_rows, tile_cols)

            @pl.when(ok)
            def _():
                hit = one_lane == ll
                at = pl.ds(lr, 1)
                count[lt, at, :] += jnp.where(hit, 1.0, 0.0)
                for n in range(steps):
                    seen[n, lt, at, :] += jnp.where(hit, obs[n, 0, o], 0.0)

            return carry

        lax.fori_loop(0, wells, well, 0)

    return pl.pallas_call(
        kernel,
        out_shape=[vmem_like(wide.shape)] + [vmem_like(big)] * 4 + [vmem_like((steps,) + big)],
        in_specs=[HBM] * 4 + [VMEM] * 2,
        out_specs=[VMEM] * 6,
        input_output_aliases={4: 0},
        scratch_shapes=[pltpu.SMEM(x.shape, x.dtype) for x in scalars]
        + [pltpu.SemaphoreType.DMA((4,))],
        compiler_params=grant(4),
        name="prepare_tile",
    )(*(in_hbm(x) for x in scalars), in_vmem(wide), in_vmem(zone_mid))


def window(prepared, scalars, row_in, col_in, xr, yr, nx, ny):
    storage, pump_rates, _, _ = scalars
    zones = storage.shape[1]
    pumps, steps = pump_rates.shape
    tiles, _, _ = big = prepared[1].shape
    own = tiles - 1
    tile_rows, tile_cols = 2 * col_in[0].shape[0], own * LANES
    assert 2 * steps + SMOOTH <= EDGE
    half = tile_rows // 2
    nxr, nyr = len(xr), len(yr)
    chunks = Chunks(tile_rows).count
    f32 = jnp.float32
    kept = len(prepared)

    def kernel(*refs):
        pos = 0

        def take(count):
            nonlocal pos
            pos += count
            return refs[pos - count : pos]

        small_in = take(2)
        pump_at = take(2)
        take(kept)
        rin, cin = take(nxr), take(nyr)
        (wide, rm, cx, cy, count, seen) = take(kept)
        smooth_out, frac_out, mat_out = take(3)
        (later, fluxx, fluxy, moved, scaled, flux, prod) = take(7)
        (px_, py_, gs_, grad, grad2) = take(5)
        (st, prs) = take(2)
        (mid_sem, small_sem) = take(2)
        res, shp, rs = wide.at[0], wide.at[1], wide.at[2]
        mat, adj, adm = wide.at[4], wide.at[5], wide.at[6]
        tx, ty = lax.axis_index("tx"), lax.axis_index("ty")
        frac = [wide.at[3]] + [later.at[n] for n in range(steps)]

        small = [
            pltpu.make_async_copy(a, b, small_sem.at[i])
            for i, (a, b) in enumerate(zip(small_in, (st, prs)))
        ]
        for copy in small:
            copy.start()
        block = (tiles, EDGE, LANES)
        zero = jnp.zeros(block, f32)
        if nxr < 2:
            for f in range(FIELDS):
                put(wide.at[f], 0, zero)
                put(wide.at[f], chunks - 1, zero)
        for ref in (
            [res, grad.at[0], grad.at[1], grad2.at[0], grad2.at[1], flux, prod]
            + frac
            + [fluxx.at[n] for n in range(steps)]
            + [scaled.at[n] for n in range(2)]
        ):
            put(ref, -1, zero)
            put(ref, chunks, zero)

        def iota(axis):
            return lax.broadcasted_iota(jnp.int32, block, axis)

        lane = iota(2)
        where_col = iota(0) * LANES + lane
        col = jnp.where(where_col < tile_cols + LANES // 2, where_col, where_col - tiles * LANES)
        gcol = col + ty * tile_cols
        total_cols, total_rows = tile_cols * ny, tile_rows * nx
        col_in_grid = (gcol >= 0) & (gcol < total_cols)
        col_face = (gcol >= 0) & (gcol + 1 < total_cols)
        row0 = tx * tile_rows - EDGE
        sub = iota(1)
        last_lane, first_lane = lane == LANES - 1, lane == 0

        def right(x):
            return turn_right(x, last_lane)

        def left(x):
            return turn_left(x, first_lane)

        one_lane = lane_iota(1, LANES)

        def number(ref, p):
            there = lax.broadcasted_iota(jnp.int32, (1, pumps), 1) == p
            return jnp.sum(jnp.where(there, ref[...], 0))

        pump_spots = [
            place_of(number(pump_at[0], p), number(pump_at[1], p), tile_rows, tile_cols)
            for p in range(pumps)
        ]

        tops = []
        for i, px in enumerate(xr):
            to = jnp.where(forward_of("tx", px), tile_rows + 2 * EDGE, EDGE)
            tops.append(pl.ds(pl.multiple_of(to, EDGE), EDGE))
            for f in range(FIELDS):
                for t in range(own):
                    wide[f, t, tops[i], :] = rin[i][
                        EDGE * f : EDGE * (f + 1), LANES * t : LANES * (t + 1)
                    ]
        edge_lane = lane_iota(EDGE, LANES)
        side = []
        for py in yr:
            low = jnp.where(forward_of("ty", py), 0, LANES - EDGE)
            side.append((edge_lane >= low) & (edge_lane < low + EDGE))

        def edge_of(messages, amount):
            out = jnp.zeros((EDGE, LANES), f32)
            for mask, message in zip(side, messages):
                part = pltpu.roll(message, (LANES - amount) % LANES, 1) if amount % LANES else message
                out = jnp.where(mask, part, out)
            return out

        for i in range(nxr):
            messages = [
                rin[i][EDGE * FIELDS :, LANES * j : LANES * (j + 1)] for j in range(nyr)
            ]
            for f in range(FIELDS):
                wide[f, own, tops[i], :] = edge_of(messages, EDGE * f)
        for h in range(2):
            for k in range(half // EDGE):
                messages = [cin[j][EDGE * k : EDGE * (k + 1), :] for j in range(nyr)]
                for f in range(FIELDS):
                    value = edge_of(messages, EDGE * f + 64 * h)
                    wide[f, own, Chunks.at(k + 1 + h * (half // EDGE)), :] = value

        def inject(k, n):
            return get(count, k) * get(frac[n], k) - get(seen.at[n - 1], k)

        for copy in small:
            copy.wait()
        tables = store_tables(st, zones)
        for k in range(chunks):
            at = Chunks.at(k)
            for t in range(0 if k in (0, chunks - 1) else own, tiles):
                res[t, at, :] = jnp.exp(-res[t, at, :])
                shp[t, at, :] = jnp.exp(shp[t, at, :])
                zone = rs[t, at, :].astype(jnp.int32)
                rs[t, at, :] = look_up(tables[0], zone)
                rm[t, at, :] = look_up(tables[1], zone)

        def row_of(k):
            return row0 + k * EDGE + sub

        ahead = {}
        for k in range(chunks + LEAD):
            if k < chunks:
                ahead[k] = right(get(res, k))
            if k < LEAD:
                continue
            j = k - LEAD
            here, at = get(res, j), Chunks.at(j)
            t = own if 0 < j < chunks - 2 else 0
            down = 2.0 / (here + get(res, j, 1))[t:]
            if t == 0:
                down = jnp.where((row_of(j) >= 0) & (row_of(j) + 1 < total_rows), down, 0.0)
            cx[t:, at, :] = down
            t = own - 1 if 0 < j < chunks - 1 else 0
            beside = 2.0 / (here + ahead.pop(j))[t:]
            cy[t:, at, :] = jnp.where(col_face[t:], beside, 0.0)

        def in_grid(k, value):
            if k in (0, chunks - 1):
                keep = col_in_grid & (row_of(k) >= 0) & (row_of(k) < total_rows)
                return jnp.where(keep, value, 0.0)
            edge = jnp.where(col_in_grid[own:], value[own:], 0.0)
            return jnp.concatenate([value[:own], edge], 0)

        for n in range(steps):
            src, dst = frac[n], frac[n + 1]
            ahead, behind = {}, {}

            def update(k, src=src, dst=dst, n=n, behind=behind):
                fx, fy, fy_left, t = behind.pop(k)
                flow = fx - get(fluxx.at[n], k, -1) + (fy - fy_left)
                put(dst, k, get(src, k) + (flow - t) * get(rs, k))

            for k in range(chunks + LEAD):
                if k < chunks:
                    ahead[k] = right(get(src, k))
                if k >= LEAD:
                    j = k - LEAD
                    f, m = get(src, j), get(mat, j)
                    fx = get(cx, j) * (get(src, j, 1) - f)
                    put(fluxx.at[n], j, fx)
                    fy = get(cy, j) * (ahead.pop(j) - f)
                    put(fluxy.at[n], j, fy)
                    t = get(shp, j) * (f - m)
                    put(moved.at[n], j, t)
                    put(mat, j, m + t * get(rm, j))
                    behind[j] = (fx, fy, left(fy), t)
                    if j >= LAG:
                        update(j - LAG)
            for j in range(chunks - LAG, chunks):
                update(j)
            for p in range(pumps):
                lr, lt, ll, ok = pump_spots[p]

                @pl.when(ok)
                def _(lr=lr, lt=lt, ll=ll, p=p, n=n, dst=dst):
                    at = pl.ds(lr, 1)
                    dst[lt, at, :] += jnp.where(one_lane == ll, prs[p, n], 0.0) * rs[lt, at, :]

        for k in range(chunks):
            a = get(adj, k) + inject(k, steps)
            put(adj, k, a)
            put(scaled.at[steps % 2], k, a * get(rs, k))
        for n in reversed(range(steps)):
            old, new = scaled.at[(n + 1) % 2], scaled.at[n % 2]
            ahead, behind, ends = {}, {}, {}

            def update(k, n=n, new=new, behind=behind):
                sx, sy, sy_left, swap = behind.pop(k)
                a = get(adj, k) + (sx - get(flux, k, -1) + (sy - sy_left)) + swap
                if n > 0:
                    a = a + inject(k, n)
                    put(new, k, a * get(rs, k))
                put(adj, k, a)

            def close(k, ends=ends):
                gx, gy, gy_left = ends.pop(k)
                total = gx + get(prod, k, -1) + (gy + gy_left)
                gc = -0.5 * get(res, k) * total
                put(grad.at[0], k, in_grid(k, gc))

            for k in range(chunks + LEAD):
                if k < chunks:
                    ahead[k] = right(get(old, k))
                if k < LEAD:
                    continue
                j = k - LEAD
                s = get(old, j)
                sx = get(cx, j) * (get(old, j, 1) - s)
                put(flux, j, sx)
                sy = get(cy, j) * (ahead.pop(j) - s)
                am = get(adm, j)
                q = am * get(rm, j) - s
                swap = get(shp, j) * q
                put(adm, j, am - swap)
                gx = get(fluxx.at[n], j) * sx
                gy = get(fluxy.at[n], j) * sy
                gs = get(moved.at[n], j) * q
                if n < steps - 1:
                    gx += get(px_, j)
                    gy += get(py_, j)
                    gs += get(gs_, j)
                behind[j] = (sx, sy, left(sy), swap)
                if n > 0:
                    put(px_, j, gx)
                    put(py_, j, gy)
                    put(gs_, j, gs)
                else:
                    put(prod, j, gx)
                    ends[j] = (gx, gy, left(gy))
                    put(grad.at[1], j, in_grid(j, gs))
                if j >= LAG:
                    update(j - LAG)
                    if n == 0:
                        close(j - LAG)
            for j in range(chunks - LAG, chunks):
                update(j)
                if n == 0:
                    close(j)

        out_copies = []
        for q, (source, out) in enumerate(((adj, frac_out), (adm, mat_out))):
            for t in range(own):
                out_copies.append(
                    pltpu.make_async_copy(
                        source.at[t, pl.ds(2 * EDGE, tile_rows)],
                        out.at[:, pl.ds(LANES * t, LANES)],
                        mid_sem.at[q, t],
                    )
                )
        for copy in out_copies:
            copy.start()

        def blur(source, ks, emit):
            turned = {}
            for i in range(len(ks) + LEAD):
                if i < len(ks):
                    g = get(source, ks[i])
                    turned[i] = left(g) + right(g)
                if i >= LEAD:
                    k = ks[i - LEAD]
                    around = get(source, k, -1) + get(source, k, 1) + turned.pop(i - LEAD)
                    emit(k, (1.0 - 4.0 * BLEND) * get(source, k) + BLEND * around)

        for q in range(2):

            def first(k, value, q=q):
                put(grad2.at[q], k, in_grid(k, value))

            blur(grad.at[q], list(range(chunks)), first)
        for q in range(2):

            def second(k, value, q=q):
                for t in range(own):
                    smooth_out[q, EDGE * (k - 1) : EDGE * k, LANES * t : LANES * (t + 1)] = value[t]

            blur(grad2.at[q], list(range(1, chunks - 1)), second)
        for copy in out_copies:
            copy.wait()

    flat = jax.ShapeDtypeStruct((tile_rows, tile_cols), f32)
    made = pl.pallas_call(
        kernel,
        out_shape=[vmem_like(x.shape) for x in prepared]
        + [vmem_like((2, tile_rows, tile_cols)), flat, flat],
        in_specs=[HBM] * 2 + [VMEM] * (2 + kept + nxr + nyr),
        out_specs=[VMEM] * (kept + 1) + [HBM] * 2,
        input_output_aliases={4 + i: i for i in range(kept)},
        scratch_shapes=[
            pltpu.VMEM((steps,) + big, f32),
            pltpu.VMEM((steps,) + big, f32),
            pltpu.VMEM((steps,) + big, f32),
            pltpu.VMEM((steps,) + big, f32),
            pltpu.VMEM((2,) + big, f32),
            pltpu.VMEM(big, f32),
            pltpu.VMEM(big, f32),
            pltpu.VMEM(big, f32),
            pltpu.VMEM(big, f32),
            pltpu.VMEM(big, f32),
            pltpu.VMEM((2,) + big, f32),
            pltpu.VMEM((2,) + big, f32),
            pltpu.SMEM(storage.shape, f32),
            pltpu.SMEM(pump_rates.shape, f32),
            pltpu.SemaphoreType.DMA((FIELDS, own)),
            pltpu.SemaphoreType.DMA((2,)),
        ],
        compiler_params=grant(24),
        name="window",
    )(
        *(in_hbm(x) for x in scalars[:2]),
        *scalars[2:],
        *(in_vmem(x) for x in list(prepared) + list(row_in) + list(col_in)),
    )
    return made[kept:]


def add_parts(mine, theirs):
    def kernel(a_ref, b_ref, cond_ref, shape_ref):
        cond_ref[...] = a_ref[0] + b_ref[0]
        shape_ref[...] = a_ref[1] + b_ref[1]

    vmem = pl.BlockSpec(memory_space=pltpu.VMEM)
    flat = jax.ShapeDtypeStruct(mine.shape[1:], mine.dtype)
    return pl.pallas_call(
        kernel, out_shape=[flat] * 2, in_specs=[vmem] * 2, out_specs=[vmem] * 2, compiler_params=grant(4), name="add_parts"
    )(in_vmem(mine), in_vmem(theirs))


def on_device(
    log_cond,
    log_shape,
    zone_ids,
    storage,
    pump_x,
    pump_y,
    pump_rates,
    obs_x,
    obs_y,
    observed,
    frac_start,
    matrix_start,
    frac_end,
    matrix_end,
):
    nx, ny = lax.axis_size("tx"), lax.axis_size("ty")
    xr, yr = rounds_of(nx), rounds_of(ny)
    fields = (
        log_cond,
        log_shape,
        zone_ids,
        frac_start[0],
        matrix_start[0],
        frac_end[0],
        matrix_end[0],
    )
    rates = jnp.transpose(pump_rates, (0, 2, 1))[0]
    seen = jnp.transpose(observed, (1, 0, 2))
    col_in, row_in = [], []
    col_out = pack_columns(fields, yr)
    for m, py in zip(col_out, yr):
        col_in.append(lax.ppermute(m, "ty", pairs_of(ny, py)))
    wide, zone_mid, row_out = load_tile(fields, xr)
    row_out = add_corners(row_out, col_in, xr)
    for m, px in zip(row_out, xr):
        row_in.append(lax.ppermute(m, "tx", pairs_of(nx, px)))
    prepared = prepare_tile(wide, zone_mid, (storage, obs_x, obs_y, seen))
    part, fracture_adj, matrix_adj = window(
        prepared, (storage, rates, pump_x, pump_y), row_in, col_in, xr, yr, nx, ny
    )
    tests = lax.axis_size("test")
    if tests == 2:
        cond_sum, shape_sum = add_parts(part, lax.ppermute(part, "test", [(0, 1), (1, 0)]))
    else:
        cond_sum, shape_sum = lax.psum(part, "test")
    return (cond_sum, shape_sum, fracture_adj[None], matrix_adj[None])


def solution(mesh):
    placed = (
        P(("inv", "tx"), "ty"),
        P(("inv", "tx"), "ty"),
        P(("inv", "tx"), "ty"),
        P("inv", None),
        P(("inv", "test"), None),
        P(("inv", "test"), None),
        P(("inv", "test"), None, None),
        P("inv"),
        P("inv"),
        P(("inv", "test"), None, None),
        P(("inv", "test"), "tx", "ty"),
        P(("inv", "test"), "tx", "ty"),
        P(("inv", "test"), "tx", "ty"),
        P(("inv", "test"), "tx", "ty"),
    )
    return jax.shard_map(
        on_device,
        mesh=mesh,
        in_specs=placed,
        out_specs=(
            P(("inv", "tx"), "ty"),
            P(("inv", "tx"), "ty"),
            P(("inv", "test"), "tx", "ty"),
            P(("inv", "test"), "tx", "ty"),
        ),
        check_vma=False,
    )
```

```python
import jax
import jax.numpy as jnp
from jax import lax
from jax.experimental import pallas as pl
from jax.experimental.pallas import tpu as pltpu
from jax.sharding import PartitionSpec as P


SMOOTH = 2
EDGE = 8
LANES = 128
BLEND = 0.2
LEAD = 6
LAG = 6
FIELDS = 7


def in_vmem(x):
    return pltpu.with_memory_space_constraint(x, pltpu.VMEM)


def in_hbm(x):
    return pltpu.with_memory_space_constraint(x, pltpu.HBM)


def pairs_of(count, parity):
    found = []
    for low in range(parity, count - 1, 2):
        found += [(low, low + 1), (low + 1, low)]
    return found


def rounds_of(count):
    return [parity for parity in (0, 1) if pairs_of(count, parity)]


def forward_of(axis, parity):
    return lax.rem(lax.axis_index(axis), 2) == parity


def lane_iota(rows, cols):
    return lax.broadcasted_iota(jnp.int32, (rows, cols), 1)


def tile_shape(fields):
    tile_rows, tile_cols = fields[0].shape
    return tile_rows, tile_cols, tile_cols // LANES


def vmem_like(shape, kind=jnp.float32):
    return pltpu.VMEM(shape, kind)


HBM = pl.BlockSpec(memory_space=pltpu.HBM)
VMEM = pl.BlockSpec(memory_space=pltpu.VMEM)


def pack_columns(fields, yr):
    tile_rows, tile_cols, _ = tile_shape(fields)
    half = tile_rows // 2
    nyr = len(yr)

    def kernel(*refs):
        ins, outs = refs[:FIELDS], refs[FIELDS : FIELDS + nyr]
        cols, zone_cols, sem = refs[FIELDS + nyr :]
        copies = []
        for j, py in enumerate(yr):
            start = jnp.where(forward_of("ty", py), tile_cols - LANES, 0)
            start = pl.multiple_of(start, LANES)
            for f in range(FIELDS):
                into = zone_cols.at[j] if f == 2 else cols.at[j, f]
                copies.append(
                    pltpu.make_async_copy(ins[f].at[:, pl.ds(start, LANES)], into, sem.at[j, f])
                )
        for copy in copies:
            copy.start()
        slot = lane_iota(EDGE, LANES) // EDGE
        for j, py in enumerate(yr):
            shift = jnp.where(forward_of("ty", py), 1, 0)
            totals = [jnp.zeros((EDGE, LANES), jnp.float32)] * (half // EDGE)
            for f in range(FIELDS):
                copies[j * FIELDS + f].wait()
                for h in range(2):
                    mask = slot == lax.rem(f + 8 * h - shift + 16, 16)
                    amount = EDGE * f + 64 * h
                    for k in range(half // EDGE):
                        at = k * EDGE + h * half
                        part = (zone_cols if f == 2 else cols.at[:, f])[j, at : at + EDGE, :]
                        part = part.astype(jnp.float32)
                        part = pltpu.roll(part, amount, 1) if amount else part
                        totals[k] = jnp.where(mask, part, totals[k])
            for k in range(half // EDGE):
                outs[j][EDGE * k : EDGE * (k + 1), :] = totals[k]

    return pl.pallas_call(
        kernel,
        out_shape=[vmem_like((half, LANES))] * nyr,
        in_specs=[HBM] * FIELDS,
        out_specs=[VMEM] * nyr,
        scratch_shapes=[
            pltpu.VMEM((nyr, FIELDS, tile_rows, LANES), jnp.float32),
            pltpu.VMEM((nyr, tile_rows, LANES), jnp.int32),
            pltpu.SemaphoreType.DMA((nyr, FIELDS)),
        ],
        compiler_params=grant(8),
        name="pack_columns",
    )(*(in_hbm(x) for x in fields))


def load_tile(fields, xr):
    tile_rows, tile_cols, own = tile_shape(fields)
    nxr = len(xr)

    def kernel(*refs):
        ins = refs[:FIELDS]
        wide, zone_mid, cx, cy = refs[FIELDS : FIELDS + 4]
        outs = refs[FIELDS + 4 : FIELDS + 4 + nxr]
        sem = refs[FIELDS + 4 + nxr]
        copies = []
        for f in range(FIELDS):
            for t in range(own):
                into = zone_mid.at[t] if f == 2 else wide.at[f, t, pl.ds(2 * EDGE, tile_rows)]
                copies.append(
                    pltpu.make_async_copy(ins[f].at[:, pl.ds(LANES * t, LANES)], into, sem.at[f, t])
                )
        for copy in copies:
            copy.start()
        for copy in copies:
            copy.wait()
        for i, px in enumerate(xr):
            start = pl.multiple_of(jnp.where(forward_of("tx", px), tile_rows - EDGE, 0), EDGE)
            for f in range(FIELDS):
                for t in range(own):
                    if f == 2:
                        part = zone_mid[t, pl.ds(start, EDGE), :].astype(jnp.float32)
                    else:
                        part = wide[f, t, pl.ds(start + 2 * EDGE, EDGE), :]
                    outs[i][EDGE * f : EDGE * (f + 1), LANES * t : LANES * (t + 1)] = part
        chunks = Chunks(tile_rows).count
        res, shp = wide.at[0], wide.at[1]
        for k in range(1, chunks - 1):
            res[0:own, Chunks.at(k), :] = jnp.exp(-res[0:own, Chunks.at(k), :])
            shp[0:own, Chunks.at(k), :] = jnp.exp(shp[0:own, Chunks.at(k), :])
        last_lane = lax.broadcasted_iota(jnp.int32, (1, EDGE, LANES), 2) == LANES - 1
        ahead = {}
        for k in range(1, chunks - 1 + LEAD):
            if k < chunks - 1:
                turned = pltpu.roll(res[0:own, Chunks.at(k), :], LANES - 1, 2)
                ahead[k] = jnp.where(last_lane, turned[1:], turned[:-1])
            j = k - LEAD
            if j >= 1:
                here = res[0:own, Chunks.at(j), :]
                if j < chunks - 2:
                    below = res[0:own, Chunks.at(j, 1), :]
                    cx[0:own, Chunks.at(j), :] = 2.0 / (here + below)
                cy[0 : own - 1, Chunks.at(j), :] = 2.0 / (here[: own - 1] + ahead.pop(j))

    big = (own + 1, tile_rows + 4 * EDGE, LANES)
    made = pl.pallas_call(
        kernel,
        out_shape=[
            vmem_like((FIELDS,) + big),
            vmem_like((own, tile_rows, LANES), jnp.int32),
            vmem_like(big),
            vmem_like(big),
        ]
        + [vmem_like((EDGE * (FIELDS + 1), tile_cols))] * nxr,
        in_specs=[HBM] * FIELDS,
        out_specs=[VMEM] * (4 + nxr),
        scratch_shapes=[pltpu.SemaphoreType.DMA((FIELDS, own))],
        compiler_params=grant(4),
        name="load_tile",
    )(*(in_hbm(x) for x in fields))
    return made[:2], made[2:4], made[4:]


def add_corners(row_out, col_in, xr):
    nxr, nyr = len(xr), len(col_in)
    assert nyr * LANES <= row_out[0].shape[1]

    def kernel(*refs):
        cols, outs = refs[:nyr], refs[nyr + nxr :]
        for i, px in enumerate(xr):
            outs[i][EDGE * FIELDS :, :] = jnp.zeros((EDGE, row_out[0].shape[1]), jnp.float32)
            ahead = forward_of("tx", px)
            for j in range(nyr):
                top = cols[j][0:EDGE, :]
                low = pltpu.roll(cols[j][cols[j].shape[0] - EDGE :, :], LANES // 2, 1)
                outs[i][EDGE * FIELDS :, LANES * j : LANES * (j + 1)] = jnp.where(ahead, low, top)

    return pl.pallas_call(
        kernel,
        out_shape=[vmem_like(x.shape) for x in row_out],
        in_specs=[VMEM] * (nyr + nxr),
        out_specs=[VMEM] * nxr,
        input_output_aliases={nyr + i: i for i in range(nxr)},
        compiler_params=grant(2),
        name="add_corners",
    )(*(in_vmem(x) for x in list(col_in) + list(row_out)))


def grant(mib):
    return pltpu.CompilerParams(vmem_limit_bytes=mib * 2**20)


class Chunks:
    def __init__(self, tile_rows):
        self.count = tile_rows // EDGE + 2

    @staticmethod
    def at(k, shift=0):
        return slice(EDGE * (k + 1) + shift, EDGE * (k + 2) + shift)


def get(ref, k, shift=0):
    return ref[:, Chunks.at(k, shift), :]


def put(ref, k, value):
    ref[:, Chunks.at(k), :] = value


def turn_right(x, last_lane):
    turned = pltpu.roll(x, LANES - 1, 2)
    return jnp.where(last_lane, jnp.concatenate([turned[1:], turned[:1]], 0), turned)


def turn_left(x, first_lane):
    turned = pltpu.roll(x, 1, 2)
    return jnp.where(first_lane, jnp.concatenate([turned[-1:], turned[:-1]], 0), turned)


def store_tables(storage_ref, zones):
    by_lane = lane_iota(EDGE, LANES)
    tables = []
    for kind in range(2):
        table = jnp.full((EDGE, LANES), storage_ref[kind, 0], jnp.float32)
        for z in range(1, zones):
            table = jnp.where(by_lane == z, storage_ref[kind, z], table)
        tables.append(1.0 / table)
    return tables


def look_up(table, index):
    return jnp.take_along_axis(table, index, axis=1, mode="promise_in_bounds")


def place_of(gx, gy, tile_rows, tile_cols):
    lr = gx - lax.axis_index("tx") * tile_rows + EDGE
    lc = gy - lax.axis_index("ty") * tile_cols
    ok = (lr >= 0) & (lr < tile_rows + 2 * EDGE) & (lc >= -EDGE) & (lc < tile_cols + EDGE)
    at = jnp.where(lc < 0, lc + tile_cols + LANES, lc)
    return lr + EDGE, at // LANES, lax.rem(at, LANES), ok


def prepare_tile(wide, zone_mid, scalars):
    storage, _, _, observed = scalars
    tile_rows = zone_mid.shape[1]
    own = zone_mid.shape[0]
    tile_cols = own * LANES
    big = wide.shape[1:]
    zones = storage.shape[1]
    steps, wells = observed.shape[0], observed.shape[2]
    chunks = Chunks(tile_rows).count
    f32 = jnp.float32

    def kernel(*refs):
        small_in, zone_in = refs[:4], refs[5]
        wide, rm, count, seen = refs[6:10]
        st, oxs, oys, obs = refs[10:14]
        sem = refs[14]
        copies = [
            pltpu.make_async_copy(a, b, sem.at[i])
            for i, (a, b) in enumerate(zip(small_in, (st, oxs, oys, obs)))
        ]
        for copy in copies:
            copy.start()
        rs = wide.at[2]
        zero = jnp.zeros((own + 1, EDGE, LANES), f32)
        for k in range(-1, chunks):
            put(count, k, zero)
            for n in range(steps):
                put(seen.at[n], k, zero)
        for copy in copies:
            copy.wait()
        tables = store_tables(st, zones)
        for k in range(1, chunks - 1):
            for t in range(own):
                zone = zone_in[t, EDGE * (k - 1) : EDGE * k, :]
                rs[t, Chunks.at(k), :] = look_up(tables[0], zone)
                rm[t, Chunks.at(k), :] = look_up(tables[1], zone)
        one_lane = lane_iota(1, LANES)

        def well(o, carry):
            lr, lt, ll, ok = place_of(oxs[o], oys[o], tile_rows, tile_cols)
            at = pl.ds(jnp.where(ok, lr, 0), 1)
            lt = jnp.where(ok, lt, 0)
            hit = one_lane == jnp.where(ok, ll, -1)
            count[lt, at, :] += jnp.where(hit, 1.0, 0.0)
            for n in range(steps):
                seen[n, lt, at, :] += jnp.where(hit, obs[n, 0, o], 0.0)
            return carry

        lax.fori_loop(0, wells, well, 0, unroll=8 if wells % 8 == 0 else 1)

    return pl.pallas_call(
        kernel,
        out_shape=[vmem_like(wide.shape)] + [vmem_like(big)] * 2 + [vmem_like((steps,) + big)],
        in_specs=[HBM] * 4 + [VMEM] * 2,
        out_specs=[VMEM] * 4,
        input_output_aliases={4: 0},
        scratch_shapes=[pltpu.SMEM(x.shape, x.dtype) for x in scalars]
        + [pltpu.SemaphoreType.DMA((4,))],
        compiler_params=grant(4),
        name="prepare_tile",
    )(*(in_hbm(x) for x in scalars), in_vmem(wide), in_vmem(zone_mid))


def masked(k, value, tile_rows, nx, ny):
    block = (1, EDGE, LANES)
    lane = lax.broadcasted_iota(jnp.int32, block, 2)
    after = jnp.where(lax.axis_index("ty") < ny - 1, 1, 0)
    before = jnp.where(lax.axis_index("ty") > 0, 1, 0)
    keep = jnp.where(lane < LANES // 2, after, before) > 0
    value = jnp.concatenate([value[:-1], jnp.where(keep, value[-1:], 0.0)], 0)
    if k in (0, tile_rows // EDGE + 1):
        tx = lax.axis_index("tx")
        value = jnp.where(tx > 0 if k == 0 else tx < nx - 1, value, 0.0)
    return value


def smooth(grad, middle, out, nx, ny):
    tile_rows = out.shape[0]
    chunks = Chunks(tile_rows).count
    lane = lax.broadcasted_iota(jnp.int32, (grad.shape[0], EDGE, LANES), 2)
    last_lane, first_lane = lane == LANES - 1, lane == 0

    def blur(source, ks, emit):
        turned = {}
        for i in range(len(ks) + LEAD):
            if i < len(ks):
                g = get(source, ks[i])
                turned[i] = turn_left(g, first_lane) + turn_right(g, last_lane)
            if i >= LEAD:
                k = ks[i - LEAD]
                around = get(source, k, -1) + get(source, k, 1) + turned.pop(i - LEAD)
                emit(k, (1.0 - 4.0 * BLEND) * get(source, k) + BLEND * around)

    def first(k, value):
        put(middle, k, masked(k, value, tile_rows, nx, ny))

    def second(k, value):
        for t in range(grad.shape[0] - 1):
            out[EDGE * (k - 1) : EDGE * k, LANES * t : LANES * (t + 1)] = value[t]

    blur(grad, list(range(chunks)), first)
    blur(middle, list(range(1, chunks - 1)), second)


def smooth_alone(grad, tile_rows, nx, ny):
    def kernel(grad_ref, out_ref, middle):
        smooth(grad_ref, middle, out_ref, nx, ny)

    tile_cols = (grad.shape[0] - 1) * LANES
    return pl.pallas_call(
        kernel,
        out_shape=vmem_like((tile_rows, tile_cols)),
        in_specs=[VMEM],
        out_specs=VMEM,
        scratch_shapes=[pltpu.VMEM(grad.shape, jnp.float32)],
        compiler_params=grant(4),
        name="smooth_alone",
    )(in_vmem(grad))


def window(prepared, scalars, row_in, col_in, xr, yr, nx, ny):
    storage, pump_rates, pump_at = scalars
    zones = storage.shape[1]
    pumps, steps = pump_rates.shape
    tiles, _, _ = big = prepared[1].shape
    own = tiles - 1
    tile_rows, tile_cols = 2 * col_in[0].shape[0], own * LANES
    assert 2 * steps + SMOOTH <= EDGE
    half = tile_rows // 2
    nxr, nyr = len(xr), len(yr)
    chunks = Chunks(tile_rows).count
    f32 = jnp.float32
    kept = len(prepared)

    def kernel(*refs):
        pos = 0

        def take(count):
            nonlocal pos
            pos += count
            return refs[pos - count : pos]

        small_in = take(3)
        take(kept)
        rin, cin = take(nxr), take(nyr)
        (wide, rm, cx, cy, count, seen) = take(kept)
        grad0, smooth_out, frac_out, mat_out = take(4)
        (later, fluxx, fluxy, moved, scaled, flux, prod) = take(7)
        (px_, py_, gs_, grad1, grad2) = take(5)
        (st, prs, spot) = take(3)
        (mid_sem, small_sem) = take(2)
        res, shp, rs = wide.at[0], wide.at[1], wide.at[2]
        mat, adj, adm = wide.at[4], wide.at[5], wide.at[6]
        tx, ty = lax.axis_index("tx"), lax.axis_index("ty")
        frac = [wide.at[3]] + [later.at[n] for n in range(steps)]

        small = [
            pltpu.make_async_copy(a, b, small_sem.at[i])
            for i, (a, b) in enumerate(zip(small_in, (st, prs, spot)))
        ]
        for copy in small:
            copy.start()
        block = (tiles, EDGE, LANES)
        zero = jnp.zeros(block, f32)
        if nxr < 2:
            for f in range(FIELDS):
                put(wide.at[f], 0, zero)
                put(wide.at[f], chunks - 1, zero)
        for ref in (
            [res, grad0, grad1, grad2, flux, prod]
            + frac
            + [fluxx.at[n] for n in range(steps)]
            + [scaled.at[n] for n in range(2)]
        ):
            put(ref, -1, zero)
            put(ref, chunks, zero)

        def iota(axis):
            return lax.broadcasted_iota(jnp.int32, block, axis)

        lane = iota(2)
        where_col = iota(0) * LANES + lane
        col = jnp.where(where_col < tile_cols + LANES // 2, where_col, where_col - tiles * LANES)
        gcol = col + ty * tile_cols
        total_cols, total_rows = tile_cols * ny, tile_rows * nx
        col_in_grid = (gcol >= 0) & (gcol < total_cols)
        col_face = (gcol >= 0) & (gcol + 1 < total_cols)
        row0 = tx * tile_rows - EDGE
        sub = iota(1)
        last_lane, first_lane = lane == LANES - 1, lane == 0

        def right(x):
            return turn_right(x, last_lane)

        def left(x):
            return turn_left(x, first_lane)

        one_lane = lane_iota(1, LANES)

        for copy in small:
            copy.wait()
        pump_spots = [
            place_of(spot[0, p], spot[0, pumps + p], tile_rows, tile_cols) for p in range(pumps)
        ]

        tops = []
        for i, px in enumerate(xr):
            to = jnp.where(forward_of("tx", px), tile_rows + 2 * EDGE, EDGE)
            tops.append(pl.ds(pl.multiple_of(to, EDGE), EDGE))
            for f in range(FIELDS):
                for t in range(own):
                    wide[f, t, tops[i], :] = rin[i][
                        EDGE * f : EDGE * (f + 1), LANES * t : LANES * (t + 1)
                    ]
        edge_lane = lane_iota(EDGE, LANES)
        side = []
        for py in yr:
            low = jnp.where(forward_of("ty", py), 0, LANES - EDGE)
            side.append((edge_lane >= low) & (edge_lane < low + EDGE))

        def edge_of(messages, amount):
            out = jnp.zeros((EDGE, LANES), f32)
            for mask, message in zip(side, messages):
                part = pltpu.roll(message, (LANES - amount) % LANES, 1) if amount % LANES else message
                out = jnp.where(mask, part, out)
            return out

        for i in range(nxr):
            messages = [
                rin[i][EDGE * FIELDS :, LANES * j : LANES * (j + 1)] for j in range(nyr)
            ]
            for f in range(FIELDS):
                wide[f, own, tops[i], :] = edge_of(messages, EDGE * f)
        for h in range(2):
            for k in range(half // EDGE):
                messages = [cin[j][EDGE * k : EDGE * (k + 1), :] for j in range(nyr)]
                for f in range(FIELDS):
                    value = edge_of(messages, EDGE * f + 64 * h)
                    wide[f, own, Chunks.at(k + 1 + h * (half // EDGE)), :] = value

        def inject(k, n):
            return get(count, k) * get(frac[n], k) - get(seen.at[n - 1], k)

        tables = store_tables(st, zones)
        for k in range(chunks):
            at = Chunks.at(k)
            for t in range(0 if k in (0, chunks - 1) else own, tiles):
                res[t, at, :] = jnp.exp(-res[t, at, :])
                shp[t, at, :] = jnp.exp(shp[t, at, :])
                zone = rs[t, at, :].astype(jnp.int32)
                rs[t, at, :] = look_up(tables[0], zone)
                rm[t, at, :] = look_up(tables[1], zone)

        def row_of(k):
            return row0 + k * EDGE + sub

        ahead = {}
        for k in range(chunks + LEAD):
            if k < chunks:
                ahead[k] = right(get(res, k))
            if k < LEAD:
                continue
            j = k - LEAD
            here, at = get(res, j), Chunks.at(j)
            t = own if 0 < j < chunks - 2 else 0
            down = 2.0 / (here + get(res, j, 1))[t:]
            if t == 0:
                down = jnp.where((row_of(j) >= 0) & (row_of(j) + 1 < total_rows), down, 0.0)
            cx[t:, at, :] = down
            t = own - 1 if 0 < j < chunks - 1 else 0
            beside = 2.0 / (here + ahead.pop(j))[t:]
            cy[t:, at, :] = jnp.where(col_face[t:], beside, 0.0)

        def in_grid(k, value):
            return masked(k, value, tile_rows, nx, ny)

        for n in range(steps):
            src, dst = frac[n], frac[n + 1]
            ahead, behind = {}, {}

            def update(k, src=src, dst=dst, n=n, behind=behind):
                fx, fy, fy_left, t = behind.pop(k)
                flow = fx - get(fluxx.at[n], k, -1) + (fy - fy_left)
                put(dst, k, get(src, k) + (flow - t) * get(rs, k))

            for k in range(chunks + LEAD):
                if k < chunks:
                    ahead[k] = right(get(src, k))
                if k >= LEAD:
                    j = k - LEAD
                    f, m = get(src, j), get(mat, j)
                    fx = get(cx, j) * (get(src, j, 1) - f)
                    put(fluxx.at[n], j, fx)
                    fy = get(cy, j) * (ahead.pop(j) - f)
                    put(fluxy.at[n], j, fy)
                    t = get(shp, j) * (f - m)
                    put(moved.at[n], j, t)
                    put(mat, j, m + t * get(rm, j))
                    behind[j] = (fx, fy, left(fy), t)
                    if j >= LAG:
                        update(j - LAG)
            for j in range(chunks - LAG, chunks):
                update(j)
            for p in range(pumps):
                lr, lt, ll, ok = pump_spots[p]

                @pl.when(ok)
                def _(lr=lr, lt=lt, ll=ll, p=p, n=n, dst=dst):
                    at = pl.ds(lr, 1)
                    dst[lt, at, :] += jnp.where(one_lane == ll, prs[p, n], 0.0) * rs[lt, at, :]

        for k in range(chunks):
            a = get(adj, k) + inject(k, steps)
            put(adj, k, a)
            put(scaled.at[steps % 2], k, a * get(rs, k))
        for n in reversed(range(steps)):
            old, new = scaled.at[(n + 1) % 2], scaled.at[n % 2]
            ahead, behind, ends = {}, {}, {}

            def update(k, n=n, new=new, behind=behind):
                sx, sy, sy_left, swap = behind.pop(k)
                a = get(adj, k) + (sx - get(flux, k, -1) + (sy - sy_left)) + swap
                if n > 0:
                    a = a + inject(k, n)
                    put(new, k, a * get(rs, k))
                put(adj, k, a)

            def close(k, ends=ends):
                gx, gy, gy_left = ends.pop(k)
                total = gx + get(prod, k, -1) + (gy + gy_left)
                gc = -0.5 * get(res, k) * total
                put(grad0, k, in_grid(k, gc))

            for k in range(chunks + LEAD):
                if k < chunks:
                    ahead[k] = right(get(old, k))
                if k < LEAD:
                    continue
                j = k - LEAD
                s = get(old, j)
                sx = get(cx, j) * (get(old, j, 1) - s)
                put(flux, j, sx)
                sy = get(cy, j) * (ahead.pop(j) - s)
                am = get(adm, j)
                q = am * get(rm, j) - s
                swap = get(shp, j) * q
                put(adm, j, am - swap)
                gx = get(fluxx.at[n], j) * sx
                gy = get(fluxy.at[n], j) * sy
                gs = get(moved.at[n], j) * q
                if n < steps - 1:
                    gx += get(px_, j)
                    gy += get(py_, j)
                    gs += get(gs_, j)
                behind[j] = (sx, sy, left(sy), swap)
                if n > 0:
                    put(px_, j, gx)
                    put(py_, j, gy)
                    put(gs_, j, gs)
                else:
                    put(prod, j, gx)
                    ends[j] = (gx, gy, left(gy))
                    put(grad1, j, in_grid(j, gs))
                if j >= LAG:
                    update(j - LAG)
                    if n == 0:
                        close(j - LAG)
            for j in range(chunks - LAG, chunks):
                update(j)
                if n == 0:
                    close(j)

        out_copies = []
        for q, (source, out) in enumerate(((adj, frac_out), (adm, mat_out))):
            for t in range(own):
                out_copies.append(
                    pltpu.make_async_copy(
                        source.at[t, pl.ds(2 * EDGE, tile_rows)],
                        out.at[:, pl.ds(LANES * t, LANES)],
                        mid_sem.at[q, t],
                    )
                )
        for copy in out_copies:
            copy.start()

        smooth(grad1, grad2, smooth_out, nx, ny)
        for copy in out_copies:
            copy.wait()

    flat = jax.ShapeDtypeStruct((tile_rows, tile_cols), f32)
    made = pl.pallas_call(
        kernel,
        out_shape=[vmem_like(x.shape) for x in prepared]
        + [vmem_like(big), vmem_like((tile_rows, tile_cols)), flat, flat],
        in_specs=[HBM] * 3 + [VMEM] * (kept + nxr + nyr),
        out_specs=[VMEM] * (kept + 2) + [HBM] * 2,
        input_output_aliases={3 + i: i for i in range(kept)},
        scratch_shapes=[
            pltpu.VMEM((steps,) + big, f32),
            pltpu.VMEM((steps,) + big, f32),
            pltpu.VMEM((steps,) + big, f32),
            pltpu.VMEM((steps,) + big, f32),
            pltpu.VMEM((2,) + big, f32),
            pltpu.VMEM(big, f32),
            pltpu.VMEM(big, f32),
            pltpu.VMEM(big, f32),
            pltpu.VMEM(big, f32),
            pltpu.VMEM(big, f32),
            pltpu.VMEM(big, f32),
            pltpu.VMEM(big, f32),
            pltpu.SMEM(storage.shape, f32),
            pltpu.SMEM(pump_rates.shape, f32),
            pltpu.SMEM(pump_at.shape, jnp.int32),
            pltpu.SemaphoreType.DMA((FIELDS, own)),
            pltpu.SemaphoreType.DMA((3,)),
        ],
        compiler_params=grant(24),
        name="window",
    )(
        *(in_hbm(x) for x in scalars),
        *(in_vmem(x) for x in list(prepared) + list(row_in) + list(col_in)),
    )
    return made[kept:]


def add_parts(mine, theirs):
    def kernel(a_ref, b_ref, out_ref):
        out_ref[...] = a_ref[...] + b_ref[...]

    flat = jax.ShapeDtypeStruct(mine.shape, mine.dtype)
    return pl.pallas_call(
        kernel,
        out_shape=flat,
        in_specs=[VMEM] * 2,
        out_specs=VMEM,
        compiler_params=grant(4),
        name="add_parts",
    )(in_vmem(mine), in_vmem(theirs))


def on_device(
    log_cond,
    log_shape,
    zone_ids,
    storage,
    pump_x,
    pump_y,
    pump_rates,
    obs_x,
    obs_y,
    observed,
    frac_start,
    matrix_start,
    frac_end,
    matrix_end,
):
    nx, ny = lax.axis_size("tx"), lax.axis_size("ty")
    xr, yr = rounds_of(nx), rounds_of(ny)
    fields = (
        log_cond,
        log_shape,
        zone_ids,
        frac_start[0],
        matrix_start[0],
        frac_end[0],
        matrix_end[0],
    )
    rates = jnp.transpose(pump_rates, (0, 2, 1))[0]
    seen = jnp.transpose(observed, (1, 0, 2))
    col_in, row_in = [], []
    col_out = pack_columns(fields, yr)
    for m, py in zip(col_out, yr):
        col_in.append(lax.ppermute(m, "ty", pairs_of(ny, py)))
    (wide, zone_mid), links, row_out = load_tile(fields, xr)
    row_out = add_corners(row_out, col_in, xr)
    for m, px in zip(row_out, xr):
        row_in.append(lax.ppermute(m, "tx", pairs_of(nx, px)))
    made = prepare_tile(wide, zone_mid, (storage, obs_x, obs_y, seen))
    prepared = list(made[:2]) + list(links) + list(made[2:])
    cond_grad, shape_part, fracture_adj, matrix_adj = window(
        prepared, (storage, rates, jnp.concatenate([pump_x, pump_y], 1)), row_in, col_in, xr, yr, nx, ny
    )
    if lax.axis_size("test") == 2:
        other = [(0, 1), (1, 0)]
        shape_other = lax.ppermute(shape_part, "test", other)
        cond_part = smooth_alone(cond_grad, log_cond.shape[0], nx, ny)
        cond_other = lax.ppermute(cond_part, "test", other)
        shape_sum = add_parts(shape_part, shape_other)
        cond_sum = add_parts(cond_part, cond_other)
    else:
        cond_part = smooth_alone(cond_grad, log_cond.shape[0], nx, ny)
        cond_sum, shape_sum = lax.psum((cond_part, shape_part), "test")
    return (cond_sum, shape_sum, fracture_adj[None], matrix_adj[None])


def solution(mesh):
    placed = (
        P(("inv", "tx"), "ty"),
        P(("inv", "tx"), "ty"),
        P(("inv", "tx"), "ty"),
        P("inv", None),
        P(("inv", "test"), None),
        P(("inv", "test"), None),
        P(("inv", "test"), None, None),
        P("inv"),
        P("inv"),
        P(("inv", "test"), None, None),
        P(("inv", "test"), "tx", "ty"),
        P(("inv", "test"), "tx", "ty"),
        P(("inv", "test"), "tx", "ty"),
        P(("inv", "test"), "tx", "ty"),
    )
    return jax.shard_map(
        on_device,
        mesh=mesh,
        in_specs=placed,
        out_specs=(
            P(("inv", "tx"), "ty"),
            P(("inv", "tx"), "ty"),
            P(("inv", "test"), "tx", "ty"),
            P(("inv", "test"), "tx", "ty"),
        ),
        check_vma=False,
    )
```

```python
import jax
import jax.numpy as jnp
from jax import lax
from jax.experimental import pallas as pl
from jax.experimental.pallas import tpu as pltpu
from jax.sharding import PartitionSpec as P


SMOOTH = 2
EDGE = 8
LANES = 128
BLEND = 0.2
LEAD = 6
LAG = 6
FIELDS = 7


def in_vmem(x):
    return pltpu.with_memory_space_constraint(x, pltpu.VMEM)


def in_hbm(x):
    return pltpu.with_memory_space_constraint(x, pltpu.HBM)


def pairs_of(count, parity):
    found = []
    for low in range(parity, count - 1, 2):
        found += [(low, low + 1), (low + 1, low)]
    return found


def rounds_of(count):
    return [parity for parity in (0, 1) if pairs_of(count, parity)]


def forward_of(axis, parity):
    return lax.rem(lax.axis_index(axis), 2) == parity


def lane_iota(rows, cols):
    return lax.broadcasted_iota(jnp.int32, (rows, cols), 1)


def tile_shape(fields):
    tile_rows, tile_cols = fields[0].shape
    return tile_rows, tile_cols, tile_cols // LANES


def vmem_like(shape, kind=jnp.float32):
    return pltpu.VMEM(shape, kind)


HBM = pl.BlockSpec(memory_space=pltpu.HBM)
VMEM = pl.BlockSpec(memory_space=pltpu.VMEM)


def pack_columns(fields, yr):
    tile_rows, tile_cols, _ = tile_shape(fields)
    half = tile_rows // 2
    nyr = len(yr)

    def kernel(*refs):
        ins, outs = refs[:FIELDS], refs[FIELDS : FIELDS + nyr]
        cols, zone_cols, sem = refs[FIELDS + nyr :]
        copies = []
        for j, py in enumerate(yr):
            start = jnp.where(forward_of("ty", py), tile_cols - LANES, 0)
            start = pl.multiple_of(start, LANES)
            for f in range(FIELDS):
                into = zone_cols.at[j] if f == 2 else cols.at[j, f]
                copies.append(
                    pltpu.make_async_copy(ins[f].at[:, pl.ds(start, LANES)], into, sem.at[j, f])
                )
        for copy in copies:
            copy.start()
        slot = lane_iota(EDGE, LANES) // EDGE
        for j, py in enumerate(yr):
            shift = jnp.where(forward_of("ty", py), 1, 0)
            totals = [jnp.zeros((EDGE, LANES), jnp.float32)] * (half // EDGE)
            for f in range(FIELDS):
                copies[j * FIELDS + f].wait()
                for h in range(2):
                    mask = slot == lax.rem(f + 8 * h - shift + 16, 16)
                    amount = EDGE * f + 64 * h
                    for k in range(half // EDGE):
                        at = k * EDGE + h * half
                        part = (zone_cols if f == 2 else cols.at[:, f])[j, at : at + EDGE, :]
                        part = part.astype(jnp.float32)
                        part = pltpu.roll(part, amount, 1) if amount else part
                        totals[k] = jnp.where(mask, part, totals[k])
            for k in range(half // EDGE):
                outs[j][EDGE * k : EDGE * (k + 1), :] = totals[k]

    return pl.pallas_call(
        kernel,
        out_shape=[vmem_like((half, LANES))] * nyr,
        in_specs=[HBM] * FIELDS,
        out_specs=[VMEM] * nyr,
        scratch_shapes=[
            pltpu.VMEM((nyr, FIELDS, tile_rows, LANES), jnp.float32),
            pltpu.VMEM((nyr, tile_rows, LANES), jnp.int32),
            pltpu.SemaphoreType.DMA((nyr, FIELDS)),
        ],
        compiler_params=grant(8),
        name="pack_columns",
    )(*(in_hbm(x) for x in fields))


def load_tile(fields, xr):
    tile_rows, tile_cols, own = tile_shape(fields)
    nxr = len(xr)

    def kernel(*refs):
        ins = refs[:FIELDS]
        wide, zone_mid, cx, cy = refs[FIELDS : FIELDS + 4]
        outs = refs[FIELDS + 4 : FIELDS + 4 + nxr]
        sem = refs[FIELDS + 4 + nxr]
        copies = []
        for f in range(FIELDS):
            for t in range(own):
                into = zone_mid.at[t] if f == 2 else wide.at[f, t, pl.ds(2 * EDGE, tile_rows)]
                copies.append(
                    pltpu.make_async_copy(ins[f].at[:, pl.ds(LANES * t, LANES)], into, sem.at[f, t])
                )
        for copy in copies:
            copy.start()
        for copy in copies:
            copy.wait()
        for i, px in enumerate(xr):
            start = pl.multiple_of(jnp.where(forward_of("tx", px), tile_rows - EDGE, 0), EDGE)
            for f in range(FIELDS):
                for t in range(own):
                    if f == 2:
                        part = zone_mid[t, pl.ds(start, EDGE), :].astype(jnp.float32)
                    else:
                        part = wide[f, t, pl.ds(start + 2 * EDGE, EDGE), :]
                    outs[i][EDGE * f : EDGE * (f + 1), LANES * t : LANES * (t + 1)] = part
        chunks = Chunks(tile_rows).count
        res, shp = wide.at[0], wide.at[1]
        for k in range(1, chunks - 1):
            res[0:own, Chunks.at(k), :] = jnp.exp(-res[0:own, Chunks.at(k), :])
            shp[0:own, Chunks.at(k), :] = jnp.exp(shp[0:own, Chunks.at(k), :])
        last_lane = lax.broadcasted_iota(jnp.int32, (1, EDGE, LANES), 2) == LANES - 1
        ahead = {}
        for k in range(1, chunks - 1 + LEAD):
            if k < chunks - 1:
                turned = pltpu.roll(res[0:own, Chunks.at(k), :], LANES - 1, 2)
                ahead[k] = jnp.where(last_lane, turned[1:], turned[:-1])
            j = k - LEAD
            if j >= 1:
                here = res[0:own, Chunks.at(j), :]
                if j < chunks - 2:
                    below = res[0:own, Chunks.at(j, 1), :]
                    cx[0:own, Chunks.at(j), :] = 2.0 / (here + below)
                cy[0 : own - 1, Chunks.at(j), :] = 2.0 / (here[: own - 1] + ahead.pop(j))

    big = (own + 1, tile_rows + 4 * EDGE, LANES)
    made = pl.pallas_call(
        kernel,
        out_shape=[
            vmem_like((FIELDS,) + big),
            vmem_like((own, tile_rows, LANES), jnp.int32),
            vmem_like(big),
            vmem_like(big),
        ]
        + [vmem_like((EDGE * (FIELDS + 1), tile_cols))] * nxr,
        in_specs=[HBM] * FIELDS,
        out_specs=[VMEM] * (4 + nxr),
        scratch_shapes=[pltpu.SemaphoreType.DMA((FIELDS, own))],
        compiler_params=grant(4),
        name="load_tile",
    )(*(in_hbm(x) for x in fields))
    return made[:2], made[2:4], made[4:]


def add_corners(row_out, col_in, xr):
    nxr, nyr = len(xr), len(col_in)
    assert nyr * LANES <= row_out[0].shape[1]

    def kernel(*refs):
        cols, outs = refs[:nyr], refs[nyr + nxr :]
        for i, px in enumerate(xr):
            outs[i][EDGE * FIELDS :, :] = jnp.zeros((EDGE, row_out[0].shape[1]), jnp.float32)
            ahead = forward_of("tx", px)
            for j in range(nyr):
                top = cols[j][0:EDGE, :]
                low = pltpu.roll(cols[j][cols[j].shape[0] - EDGE :, :], LANES // 2, 1)
                outs[i][EDGE * FIELDS :, LANES * j : LANES * (j + 1)] = jnp.where(ahead, low, top)

    return pl.pallas_call(
        kernel,
        out_shape=[vmem_like(x.shape) for x in row_out],
        in_specs=[VMEM] * (nyr + nxr),
        out_specs=[VMEM] * nxr,
        input_output_aliases={nyr + i: i for i in range(nxr)},
        compiler_params=grant(2),
        name="add_corners",
    )(*(in_vmem(x) for x in list(col_in) + list(row_out)))


def grant(mib):
    return pltpu.CompilerParams(vmem_limit_bytes=mib * 2**20)


class Chunks:
    def __init__(self, tile_rows):
        self.count = tile_rows // EDGE + 2

    @staticmethod
    def at(k, shift=0):
        return slice(EDGE * (k + 1) + shift, EDGE * (k + 2) + shift)


def get(ref, k, shift=0):
    return ref[:, Chunks.at(k, shift), :]


def put(ref, k, value):
    ref[:, Chunks.at(k), :] = value


def turn_right(x, last_lane):
    turned = pltpu.roll(x, LANES - 1, 2)
    return jnp.where(last_lane, jnp.concatenate([turned[1:], turned[:1]], 0), turned)


def turn_left(x, first_lane):
    turned = pltpu.roll(x, 1, 2)
    return jnp.where(first_lane, jnp.concatenate([turned[-1:], turned[:-1]], 0), turned)


def store_tables(storage_ref, zones):
    by_lane = lane_iota(EDGE, LANES)
    tables = []
    for kind in range(2):
        table = jnp.full((EDGE, LANES), storage_ref[kind, 0], jnp.float32)
        for z in range(1, zones):
            table = jnp.where(by_lane == z, storage_ref[kind, z], table)
        tables.append(1.0 / table)
    return tables


def look_up(table, index):
    return jnp.take_along_axis(table, index, axis=1, mode="promise_in_bounds")


def place_of(gx, gy, tile_rows, tile_cols):
    lr = gx - lax.axis_index("tx") * tile_rows + EDGE
    lc = gy - lax.axis_index("ty") * tile_cols
    ok = (lr >= 0) & (lr < tile_rows + 2 * EDGE) & (lc >= -EDGE) & (lc < tile_cols + EDGE)
    at = jnp.where(lc < 0, lc + tile_cols + LANES, lc)
    return lr + EDGE, at // LANES, lax.rem(at, LANES), ok


def edge_sides(yr):
    lane = lane_iota(EDGE, LANES)
    side = []
    for py in yr:
        low = jnp.where(forward_of("ty", py), 0, LANES - EDGE)
        side.append((lane >= low) & (lane < low + EDGE))
    return side


def edge_of(side, messages, amount):
    out = jnp.zeros((EDGE, LANES), jnp.float32)
    for mask, message in zip(side, messages):
        part = pltpu.roll(message, (LANES - amount) % LANES, 1) if amount % LANES else message
        out = jnp.where(mask, part, out)
    return out


def column_faces(tiles, ny):
    block = (tiles, EDGE, LANES)
    at = lax.broadcasted_iota(jnp.int32, block, 0) * LANES + lax.broadcasted_iota(jnp.int32, block, 2)
    tile_cols = (tiles - 1) * LANES
    col = jnp.where(at < tile_cols + LANES // 2, at, at - tiles * LANES)
    col = col + lax.axis_index("ty") * tile_cols
    return (col >= 0) & (col + 1 < tile_cols * ny)


def prepare_tile(wide, zone_mid, links, col_in, scalars, yr, ny):
    storage, _, _, observed = scalars
    tile_rows = zone_mid.shape[1]
    own = zone_mid.shape[0]
    tile_cols = own * LANES
    big = wide.shape[1:]
    zones = storage.shape[1]
    steps, wells = observed.shape[0], observed.shape[2]
    half, nyr = tile_rows // 2, len(yr)
    chunks = Chunks(tile_rows).count
    f32 = jnp.float32

    def kernel(*refs):
        small_in, zone_in, cin = refs[:4], refs[5], refs[8 : 8 + nyr]
        wide, rm, cx, cy, count, seen = refs[8 + nyr : 14 + nyr]
        st, oxs, oys, obs = refs[14 + nyr : 18 + nyr]
        sem = refs[18 + nyr]
        copies = [
            pltpu.make_async_copy(a, b, sem.at[i])
            for i, (a, b) in enumerate(zip(small_in, (st, oxs, oys, obs)))
        ]
        for copy in copies:
            copy.start()
        rs = wide.at[2]
        zero = jnp.zeros((own + 1, EDGE, LANES), f32)
        for k in range(-1, chunks):
            put(count, k, zero)
            for n in range(steps):
                put(seen.at[n], k, zero)
        side = edge_sides(yr)
        for h in range(2):
            for k in range(half // EDGE):
                messages = [cin[j][EDGE * k : EDGE * (k + 1), :] for j in range(nyr)]
                for f in range(FIELDS):
                    value = edge_of(side, messages, EDGE * f + 64 * h)
                    value = jnp.exp(-value) if f == 0 else jnp.exp(value) if f == 1 else value
                    wide[f, own, Chunks.at(k + 1 + h * (half // EDGE)), :] = value
        res = wide.at[0]
        last_lane = lax.broadcasted_iota(jnp.int32, (own + 1, EDGE, LANES), 2) == LANES - 1
        faces = column_faces(own + 1, ny)
        ahead = {}
        for k in range(1, chunks - 1 + LEAD):
            if k < chunks - 1:
                ahead[k] = turn_right(get(res, k), last_lane)[own - 1 :]
            j = k - LEAD
            if j >= 1:
                here, at = get(res, j)[own - 1 :], Chunks.at(j)
                if j < chunks - 2:
                    cx[own, at, :] = 2.0 / (here[1] + res[own, Chunks.at(j, 1), :])
                beside = 2.0 / (here + ahead.pop(j))
                cy[own - 1 :, at, :] = jnp.where(faces[own - 1 :], beside, 0.0)
        for copy in copies:
            copy.wait()
        tables = store_tables(st, zones)
        for k in range(1, chunks - 1):
            for t in range(own + 1):
                if t < own:
                    zone = zone_in[t, EDGE * (k - 1) : EDGE * k, :]
                else:
                    zone = rs[t, Chunks.at(k), :].astype(jnp.int32)
                rs[t, Chunks.at(k), :] = look_up(tables[0], zone)
                rm[t, Chunks.at(k), :] = look_up(tables[1], zone)
        one_lane = lane_iota(1, LANES)

        def well(o, carry):
            lr, lt, ll, ok = place_of(oxs[o], oys[o], tile_rows, tile_cols)
            at = pl.ds(jnp.where(ok, lr, 0), 1)
            lt = jnp.where(ok, lt, 0)
            hit = one_lane == jnp.where(ok, ll, -1)
            old = [count[lt, at, :]] + [seen[n, lt, at, :] for n in range(steps)]
            count[lt, at, :] = old[0] + jnp.where(hit, 1.0, 0.0)
            for n in range(steps):
                seen[n, lt, at, :] = old[n + 1] + jnp.where(hit, obs[n, 0, o], 0.0)
            return carry

        lax.fori_loop(0, wells, well, 0, unroll=wells)

    return pl.pallas_call(
        kernel,
        out_shape=[vmem_like(wide.shape)] + [vmem_like(big)] * 4 + [vmem_like((steps,) + big)],
        in_specs=[HBM] * 4 + [VMEM] * (4 + nyr),
        out_specs=[VMEM] * 6,
        input_output_aliases={4: 0, 6: 2, 7: 3},
        scratch_shapes=[pltpu.SMEM(x.shape, x.dtype) for x in scalars]
        + [pltpu.SemaphoreType.DMA((4,))],
        compiler_params=grant(4),
        name="prepare_tile",
    )(
        *(in_hbm(x) for x in scalars),
        *(in_vmem(x) for x in [wide, zone_mid] + list(links) + list(col_in)),
    )


def masked(k, value, tile_rows, nx, ny):
    block = (1, EDGE, LANES)
    lane = lax.broadcasted_iota(jnp.int32, block, 2)
    after = jnp.where(lax.axis_index("ty") < ny - 1, 1, 0)
    before = jnp.where(lax.axis_index("ty") > 0, 1, 0)
    keep = jnp.where(lane < LANES // 2, after, before) > 0
    value = jnp.concatenate([value[:-1], jnp.where(keep, value[-1:], 0.0)], 0)
    if k in (0, tile_rows // EDGE + 1):
        tx = lax.axis_index("tx")
        value = jnp.where(tx > 0 if k == 0 else tx < nx - 1, value, 0.0)
    return value


def smooth(grad, middle, out, nx, ny):
    tile_rows = out.shape[0]
    chunks = Chunks(tile_rows).count
    lane = lax.broadcasted_iota(jnp.int32, (grad.shape[0], EDGE, LANES), 2)
    last_lane, first_lane = lane == LANES - 1, lane == 0

    def blur(source, ks, emit):
        turned = {}
        for i in range(len(ks) + LEAD):
            if i < len(ks):
                g = get(source, ks[i])
                turned[i] = turn_left(g, first_lane) + turn_right(g, last_lane)
            if i >= LEAD:
                k = ks[i - LEAD]
                around = get(source, k, -1) + get(source, k, 1) + turned.pop(i - LEAD)
                emit(k, get(source, k) + around)

    def first(k, value):
        put(middle, k, masked(k, value, tile_rows, nx, ny))

    def second(k, value):
        for t in range(grad.shape[0] - 1):
            out[EDGE * (k - 1) : EDGE * k, LANES * t : LANES * (t + 1)] = (BLEND * BLEND) * value[t]

    blur(grad, list(range(chunks)), first)
    blur(middle, list(range(1, chunks - 1)), second)


def smooth_alone(grad, tile_rows, nx, ny):
    def kernel(grad_ref, out_ref, middle):
        smooth(grad_ref, middle, out_ref, nx, ny)

    tile_cols = (grad.shape[0] - 1) * LANES
    return pl.pallas_call(
        kernel,
        out_shape=vmem_like((tile_rows, tile_cols)),
        in_specs=[VMEM],
        out_specs=VMEM,
        scratch_shapes=[pltpu.VMEM(grad.shape, jnp.float32)],
        compiler_params=grant(4),
        name="smooth_alone",
    )(in_vmem(grad))


def window(prepared, scalars, row_in, col_in, xr, yr, nx, ny):
    storage, pump_rates, pump_at = scalars
    zones = storage.shape[1]
    pumps, steps = pump_rates.shape
    tiles, _, _ = big = prepared[1].shape
    own = tiles - 1
    tile_rows, tile_cols = 2 * col_in[0].shape[0], own * LANES
    assert 2 * steps + SMOOTH <= EDGE
    nxr, nyr = len(xr), len(yr)
    chunks = Chunks(tile_rows).count
    f32 = jnp.float32
    kept = len(prepared)

    def kernel(*refs):
        pos = 0

        def take(count):
            nonlocal pos
            pos += count
            return refs[pos - count : pos]

        small_in = take(3)
        take(kept)
        rin, cin = take(nxr), take(nyr)
        (wide, rm, cx, cy, count, seen) = take(kept)
        grad0, smooth_out, frac_out, mat_out = take(4)
        (later, fluxx, fluxy, moved, scaled, flux, prod) = take(7)
        (px_, py_, gs_, grad1, grad2) = take(5)
        (st, prs, spot) = take(3)
        (mid_sem, small_sem) = take(2)
        res, shp, rs = wide.at[0], wide.at[1], wide.at[2]
        mat, adj, adm = wide.at[4], wide.at[5], wide.at[6]
        tx = lax.axis_index("tx")
        frac = [wide.at[3]] + [later.at[n] for n in range(steps)]

        small = [
            pltpu.make_async_copy(a, b, small_sem.at[i])
            for i, (a, b) in enumerate(zip(small_in, (st, prs, spot)))
        ]
        for copy in small:
            copy.start()
        block = (tiles, EDGE, LANES)
        zero = jnp.zeros(block, f32)
        if nxr < 2:
            for f in range(FIELDS):
                put(wide.at[f], 0, zero)
                put(wide.at[f], chunks - 1, zero)
        for ref in (
            [res, grad0, grad1, grad2, flux, prod]
            + frac
            + [fluxx.at[n] for n in range(steps)]
            + [scaled.at[n] for n in range(2)]
        ):
            put(ref, -1, zero)
            put(ref, chunks, zero)

        def iota(axis):
            return lax.broadcasted_iota(jnp.int32, block, axis)

        lane = iota(2)
        total_rows = tile_rows * nx
        col_face = column_faces(tiles, ny)
        row0 = tx * tile_rows - EDGE
        sub = iota(1)
        last_lane, first_lane = lane == LANES - 1, lane == 0

        def right(x):
            return turn_right(x, last_lane)

        def left(x):
            return turn_left(x, first_lane)

        one_lane = lane_iota(1, LANES)

        for copy in small:
            copy.wait()
        pump_spots = [
            place_of(spot[0, p], spot[0, pumps + p], tile_rows, tile_cols) for p in range(pumps)
        ]

        tops = []
        for i, px in enumerate(xr):
            to = jnp.where(forward_of("tx", px), tile_rows + 2 * EDGE, EDGE)
            tops.append(pl.ds(pl.multiple_of(to, EDGE), EDGE))
            for f in range(FIELDS):
                for t in range(own):
                    wide[f, t, tops[i], :] = rin[i][
                        EDGE * f : EDGE * (f + 1), LANES * t : LANES * (t + 1)
                    ]
        side = edge_sides(yr)
        for i in range(nxr):
            messages = [
                rin[i][EDGE * FIELDS :, LANES * j : LANES * (j + 1)] for j in range(nyr)
            ]
            for f in range(FIELDS):
                wide[f, own, tops[i], :] = edge_of(side, messages, EDGE * f)

        def inject(k, n):
            return get(count, k) * get(frac[n], k) - get(seen.at[n - 1], k)

        tables = store_tables(st, zones)
        for k in (0, chunks - 1):
            at = Chunks.at(k)
            for t in range(tiles):
                res[t, at, :] = jnp.exp(-res[t, at, :])
                shp[t, at, :] = jnp.exp(shp[t, at, :])
                zone = rs[t, at, :].astype(jnp.int32)
                rs[t, at, :] = look_up(tables[0], zone)
                rm[t, at, :] = look_up(tables[1], zone)

        def row_of(k):
            return row0 + k * EDGE + sub

        for k in (0, chunks - 2, chunks - 1):
            here = get(res, k)
            down = 2.0 / (here + get(res, k, 1))
            put(cx, k, jnp.where((row_of(k) >= 0) & (row_of(k) + 1 < total_rows), down, 0.0))
            if k != chunks - 2:
                put(cy, k, jnp.where(col_face, 2.0 / (here + right(here)), 0.0))

        def in_grid(k, value):
            return masked(k, value, tile_rows, nx, ny)

        for n in range(steps):
            src, dst = frac[n], frac[n + 1]
            ahead, behind = {}, {}

            def update(k, src=src, dst=dst, n=n, behind=behind):
                fx, fy, fy_left, t = behind.pop(k)
                flow = fx - get(fluxx.at[n], k, -1) + (fy - fy_left)
                put(dst, k, get(src, k) + (flow - t) * get(rs, k))

            for k in range(chunks + LEAD):
                if k < chunks:
                    ahead[k] = right(get(src, k))
                if k >= LEAD:
                    j = k - LEAD
                    f, m = get(src, j), get(mat, j)
                    fx = get(cx, j) * (get(src, j, 1) - f)
                    put(fluxx.at[n], j, fx)
                    fy = get(cy, j) * (ahead.pop(j) - f)
                    put(fluxy.at[n], j, fy)
                    t = get(shp, j) * (f - m)
                    put(moved.at[n], j, t)
                    put(mat, j, m + t * get(rm, j))
                    behind[j] = (fx, fy, left(fy), t)
                    if j >= LAG:
                        update(j - LAG)
            for j in range(chunks - LAG, chunks):
                update(j)
            for p in range(pumps):
                lr, lt, ll, ok = pump_spots[p]

                @pl.when(ok)
                def _(lr=lr, lt=lt, ll=ll, p=p, n=n, dst=dst):
                    at = pl.ds(lr, 1)
                    dst[lt, at, :] += jnp.where(one_lane == ll, prs[p, n], 0.0) * rs[lt, at, :]

        for k in range(chunks):
            a = get(adj, k) + inject(k, steps)
            put(adj, k, a)
            put(scaled.at[steps % 2], k, a * get(rs, k))
        for n in reversed(range(steps)):
            old, new = scaled.at[(n + 1) % 2], scaled.at[n % 2]
            ahead, behind, ends = {}, {}, {}

            def update(k, n=n, new=new, behind=behind):
                sx, sy, sy_left, swap = behind.pop(k)
                a = get(adj, k) + (sx - get(flux, k, -1) + (sy - sy_left)) + swap
                if n > 0:
                    a = a + inject(k, n)
                    put(new, k, a * get(rs, k))
                put(adj, k, a)

            def close(k, ends=ends):
                gx, gy, gy_left = ends.pop(k)
                total = gx + get(prod, k, -1) + (gy + gy_left)
                gc = -0.5 * get(res, k) * total
                put(grad0, k, in_grid(k, gc))

            for k in range(chunks + LEAD):
                if k < chunks:
                    ahead[k] = right(get(old, k))
                if k < LEAD:
                    continue
                j = k - LEAD
                s = get(old, j)
                sx = get(cx, j) * (get(old, j, 1) - s)
                put(flux, j, sx)
                sy = get(cy, j) * (ahead.pop(j) - s)
                am = get(adm, j)
                q = am * get(rm, j) - s
                swap = get(shp, j) * q
                put(adm, j, am - swap)
                gx = get(fluxx.at[n], j) * sx
                gy = get(fluxy.at[n], j) * sy
                gs = get(moved.at[n], j) * q
                if n < steps - 1:
                    gx += get(px_, j)
                    gy += get(py_, j)
                    gs += get(gs_, j)
                behind[j] = (sx, sy, left(sy), swap)
                if n > 0:
                    put(px_, j, gx)
                    put(py_, j, gy)
                    put(gs_, j, gs)
                else:
                    put(prod, j, gx)
                    ends[j] = (gx, gy, left(gy))
                    put(grad1, j, in_grid(j, gs))
                if j >= LAG:
                    update(j - LAG)
                    if n == 0:
                        close(j - LAG)
            for j in range(chunks - LAG, chunks):
                update(j)
                if n == 0:
                    close(j)

        out_copies = []
        for q, (source, out) in enumerate(((adj, frac_out), (adm, mat_out))):
            for t in range(own):
                out_copies.append(
                    pltpu.make_async_copy(
                        source.at[t, pl.ds(2 * EDGE, tile_rows)],
                        out.at[:, pl.ds(LANES * t, LANES)],
                        mid_sem.at[q, t],
                    )
                )
        for copy in out_copies:
            copy.start()

        smooth(grad1, grad2, smooth_out, nx, ny)
        for copy in out_copies:
            copy.wait()

    flat = jax.ShapeDtypeStruct((tile_rows, tile_cols), f32)
    made = pl.pallas_call(
        kernel,
        out_shape=[vmem_like(x.shape) for x in prepared]
        + [vmem_like(big), vmem_like((tile_rows, tile_cols)), flat, flat],
        in_specs=[HBM] * 3 + [VMEM] * (kept + nxr + nyr),
        out_specs=[VMEM] * (kept + 2) + [HBM] * 2,
        input_output_aliases={3 + i: i for i in range(kept)},
        scratch_shapes=[
            pltpu.VMEM((steps,) + big, f32),
            pltpu.VMEM((steps,) + big, f32),
            pltpu.VMEM((steps,) + big, f32),
            pltpu.VMEM((steps,) + big, f32),
            pltpu.VMEM((2,) + big, f32),
            pltpu.VMEM(big, f32),
            pltpu.VMEM(big, f32),
            pltpu.VMEM(big, f32),
            pltpu.VMEM(big, f32),
            pltpu.VMEM(big, f32),
            pltpu.VMEM(big, f32),
            pltpu.VMEM(big, f32),
            pltpu.SMEM(storage.shape, f32),
            pltpu.SMEM(pump_rates.shape, f32),
            pltpu.SMEM(pump_at.shape, jnp.int32),
            pltpu.SemaphoreType.DMA((FIELDS, own)),
            pltpu.SemaphoreType.DMA((3,)),
        ],
        compiler_params=grant(24),
        name="window",
    )(
        *(in_hbm(x) for x in scalars),
        *(in_vmem(x) for x in list(prepared) + list(row_in) + list(col_in)),
    )
    return made[kept:]


def add_parts(mine, theirs):
    def kernel(a_ref, b_ref, out_ref):
        out_ref[...] = a_ref[...] + b_ref[...]

    flat = jax.ShapeDtypeStruct(mine.shape, mine.dtype)
    return pl.pallas_call(
        kernel,
        out_shape=flat,
        in_specs=[VMEM] * 2,
        out_specs=VMEM,
        compiler_params=grant(4),
        name="add_parts",
    )(in_vmem(mine), in_vmem(theirs))


def on_device(
    log_cond,
    log_shape,
    zone_ids,
    storage,
    pump_x,
    pump_y,
    pump_rates,
    obs_x,
    obs_y,
    observed,
    frac_start,
    matrix_start,
    frac_end,
    matrix_end,
):
    nx, ny = lax.axis_size("tx"), lax.axis_size("ty")
    xr, yr = rounds_of(nx), rounds_of(ny)
    fields = (
        log_cond,
        log_shape,
        zone_ids,
        frac_start[0],
        matrix_start[0],
        frac_end[0],
        matrix_end[0],
    )
    rates = jnp.transpose(pump_rates, (0, 2, 1))[0]
    seen = jnp.transpose(observed, (1, 0, 2))
    col_in, row_in = [], []
    col_out = pack_columns(fields, yr)
    for m, py in zip(col_out, yr):
        col_in.append(lax.ppermute(m, "ty", pairs_of(ny, py)))
    (wide, zone_mid), links, row_out = load_tile(fields, xr)
    row_out = add_corners(row_out, col_in, xr)
    for m, px in zip(row_out, xr):
        row_in.append(lax.ppermute(m, "tx", pairs_of(nx, px)))
    prepared = prepare_tile(wide, zone_mid, links, col_in, (storage, obs_x, obs_y, seen), yr, ny)
    cond_grad, shape_part, fracture_adj, matrix_adj = window(
        prepared, (storage, rates, jnp.concatenate([pump_x, pump_y], 1)), row_in, col_in, xr, yr, nx, ny
    )
    if lax.axis_size("test") == 2:
        other = [(0, 1), (1, 0)]
        shape_other = lax.ppermute(shape_part, "test", other)
        cond_part = smooth_alone(cond_grad, log_cond.shape[0], nx, ny)
        cond_other = lax.ppermute(cond_part, "test", other)
        shape_sum = add_parts(shape_part, shape_other)
        cond_sum = add_parts(cond_part, cond_other)
    else:
        cond_part = smooth_alone(cond_grad, log_cond.shape[0], nx, ny)
        cond_sum, shape_sum = lax.psum((cond_part, shape_part), "test")
    return (cond_sum, shape_sum, fracture_adj[None], matrix_adj[None])


def solution(mesh):
    placed = (
        P(("inv", "tx"), "ty"),
        P(("inv", "tx"), "ty"),
        P(("inv", "tx"), "ty"),
        P("inv", None),
        P(("inv", "test"), None),
        P(("inv", "test"), None),
        P(("inv", "test"), None, None),
        P("inv"),
        P("inv"),
        P(("inv", "test"), None, None),
        P(("inv", "test"), "tx", "ty"),
        P(("inv", "test"), "tx", "ty"),
        P(("inv", "test"), "tx", "ty"),
        P(("inv", "test"), "tx", "ty"),
    )
    return jax.shard_map(
        on_device,
        mesh=mesh,
        in_specs=placed,
        out_specs=(
            P(("inv", "tx"), "ty"),
            P(("inv", "tx"), "ty"),
            P(("inv", "test"), "tx", "ty"),
            P(("inv", "test"), "tx", "ty"),
        ),
        check_vma=False,
    )
```
